256 devices in a mesh: gx: 32 (over y, z_lo, x), gy: 8 (over z_hi, core).
Axes of the slice: x: 4, y: 4, z: 8 (z_hi: 4, z_lo: 2; z = z_hi * 2 + z_lo), core: 2. Of those that a mesh axis runs over, the one named last changes fastest.
Arguments:
- hidden: bfloat16 [2240, 5120], P('gy', 'gx'), may hold values from -6 to 6
- norm_gain: float32 [5120], P('gx'), may hold values from 0.1 to 1.9
- qkv_weight: bfloat16 [5120, 7168], P('gx', 'gy'), may hold values from -0.078125 to 0.078125
- qkv_bias: bfloat16 [7168], P('gy'), may hold values from -5 to 5
- out_weight: bfloat16 [5120, 5120], P('gy', 'gx'), may hold values from -0.078125 to 0.078125
- key_cache: bfloat16 [5, 8704, 1024], P(None, 'gx', 'gy'), may hold values from -68 to 68
- value_cache: bfloat16 [5, 8704, 1024], P(None, 'gx', 'gy'), may hold values from -12 to 12
- cached_len: int32 [5], replicated, may hold values from 1 to 8192, as said below
- fresh_len: int32 [5], replicated, may hold values from 224 to 448, as said below
Outputs:
- output: bfloat16 [2240, 5120], P('gy', 'gx')
- key_out: bfloat16 [5, 8704, 1024], P(None, 'gx', 'gy')
- value_out: bfloat16 [5, 8704, 1024], P(None, 'gx', 'gy')
The draws below stay inside these ranges and needn't reach their ends.
Inputs may be any that keep to these rules, and one draw needn't show every extreme that they name: `cached_len`: two requests have 8192 - 8192 // 32 or more cached tokens, one of them exactly 8192; the other three fewer than 256. `fresh_len`: one request has exactly 448 live new tokens.
All inputs are finite; a program needn't handle non-finite values.
Results may differ from the reference program's by a relative error of at most 0.012.
Values may be sent and summed in bfloat16 or wider, within the bound.
A program may use at most 128 MiB of HBM per device.

```python
import jax
import jax.numpy as jnp
from jax import lax

D = 5120
HEADS = 40
KV_HEADS = 8
HEAD_DIM = 128
GROUP = 5
REQUESTS = 5
NEW_TOKENS = 448
CACHED_MAX = 8192
TOKENS = 2240
CAPACITY = 8704


def draw_cached_len(key, part):
    short_top = CACHED_MAX // 32
    first, second, third = jax.random.split(jax.random.fold_in(key, 11), 3)
    lengths = jax.random.randint(first, (REQUESTS,), 1, short_top)
    order = jax.random.permutation(second, REQUESTS)
    near = jax.random.randint(third, (), CACHED_MAX - short_top, CACHED_MAX + 1)
    lengths = lengths.at[order[0]].set(CACHED_MAX)
    lengths = lengths.at[order[1]].set(near)
    return lengths.astype(jnp.int32)


def draw_fresh_len(key, part):
    first, second = jax.random.split(jax.random.fold_in(key, 23))
    lengths = jax.random.randint(first, (REQUESTS,), NEW_TOKENS // 2, NEW_TOKENS + 1)
    chosen = jax.random.randint(second, (), 0, REQUESTS)
    lengths = lengths.at[chosen].set(NEW_TOKENS)
    return lengths.astype(jnp.int32)


def draw_key_cache(key, part):
    first = jax.random.fold_in(jax.random.fold_in(key, 37), 0)
    shape = (REQUESTS, CAPACITY, KV_HEADS * HEAD_DIM)
    return jnp.clip(jax.random.normal(first, shape, jnp.float32), -4.0, 4.0).astype(jnp.bfloat16)


def draw_value_cache(key, part):
    first = jax.random.fold_in(jax.random.fold_in(key, 53), 0)
    shape = (REQUESTS, CAPACITY, KV_HEADS * HEAD_DIM)
    rise = jnp.arange(CAPACITY, dtype=jnp.float32) / CAPACITY
    base = jnp.clip(jax.random.normal(first, shape, jnp.float32), -4.0, 4.0)
    return (base * (1.0 + 2.0 * rise)[None, :, None]).astype(jnp.bfloat16)


def steps_of(rng, dims, cuts, smallest, top_value):
    level = 1.0
    for axis_at, blocks in cuts:
        draws = jax.random.uniform(jax.random.fold_in(jax.random.fold_in(rng, 6), axis_at), (blocks,), jnp.float32, smallest / len(cuts), top_value / len(cuts))
        level = level * jnp.repeat(jnp.exp(draws), dims[axis_at] // blocks).reshape((-1,) + (1,) * (len(dims) - 1 - axis_at))
    return level


def gaussian(key, dims, width, bound, cuts=(), kind=jnp.bfloat16):
    gain = steps_of(key, dims, cuts, -0.22, 0.18) if cuts else 1.0
    entries = jax.random.normal(key, dims, jnp.float32) * width * gain
    return jnp.minimum(jnp.maximum(entries, -bound), bound).astype(kind)


def setup_inputs(seed: int = 0) -> dict:
    keys = jax.random.split(jax.random.key(seed), 10)
    return {
        "hidden": gaussian(keys[0], (TOKENS, D), 1.0, 6.0, ((0, 8), (1, 32))),
        "norm_gain": jnp.clip(1.0 + 0.18 * jax.random.normal(keys[1], (D,), jnp.float32), 0.1, 1.9),
        "qkv_weight": gaussian(keys[2], (D, KV_HEADS * (GROUP + 2) * HEAD_DIM), D ** -0.5, 0.078125, ((0, 32), (1, 8))),
        "qkv_bias": gaussian(keys[3], (KV_HEADS * (GROUP + 2) * HEAD_DIM,), 1.0, 5.0, ((0, 8),)),
        "out_weight": gaussian(keys[4], (HEADS * HEAD_DIM, D), (HEADS * HEAD_DIM) ** -0.5, 0.078125, ((0, 8), (1, 32))),
        "key_cache": draw_key_cache(jax.random.fold_in(keys[9], 71), 0),
        "value_cache": draw_value_cache(jax.random.fold_in(keys[9], 71), 0),
        "cached_len": draw_cached_len(jax.random.fold_in(keys[9], 71), 0),
        "fresh_len": draw_fresh_len(jax.random.fold_in(keys[9], 71), 0),
    }


ROPE_THETA = 1000000.0
NORM_EPS = 1e-06
NEG_LARGE = -1e+30

def rotate(vectors, positions):
    half_dim = vectors.shape[-1] // 2
    exponent = jnp.arange(half_dim, dtype=jnp.int32).astype(jnp.float32) * (2.0 / vectors.shape[-1])
    frequency = 1.0 / ROPE_THETA ** exponent
    angles = positions[:, None] * frequency[None, :]
    target = (positions.shape[0],) + (1,) * (vectors.ndim - 2) + (half_dim,)
    cos_table = jnp.cos(angles).reshape(target)
    sin_table = jnp.sin(angles).reshape(target)
    first_half = vectors[..., :half_dim]
    second_half = vectors[..., half_dim:]
    return jnp.concatenate([first_half * cos_table - second_half * sin_table, second_half * cos_table + first_half * sin_table], -1)

def token_positions(cached_len, fresh_len, first_row, row_count):
    rows_here = first_row + jnp.arange(row_count, dtype=jnp.int32)
    request = rows_here // NEW_TOKENS
    within = rows_here % NEW_TOKENS
    picked = request[:, None] == jnp.arange(REQUESTS, dtype=jnp.int32)[None, :]
    start_pos = lax.optimization_barrier(jnp.sum(jnp.where(picked, cached_len[None, :], 0), 1))
    live_count = lax.optimization_barrier(jnp.sum(jnp.where(picked, fresh_len[None, :], 0), 1))
    return ((start_pos + within).astype(jnp.int32), within < live_count)

def finish_rows(projected, cached_len, fresh_len, first_row):
    row_count = projected.shape[0]
    groups_here = projected.shape[1] // ((GROUP + 2) * HEAD_DIM)
    shaped = projected.reshape(row_count, groups_here, GROUP + 2, HEAD_DIM)
    positions, unused_live = token_positions(cached_len, fresh_len, first_row, row_count)
    angle_pos = positions.astype(jnp.float32)
    queries = rotate(shaped[:, :, :GROUP], angle_pos).astype(jnp.bfloat16).reshape(row_count, -1)
    new_keys = rotate(shaped[:, :, GROUP], angle_pos).astype(jnp.bfloat16).reshape(row_count, -1)
    new_values = shaped[:, :, GROUP + 1].astype(jnp.bfloat16).reshape(row_count, -1)
    return (queries, new_keys, new_values)

def append_rows(cache, new_rows, cached_len, fresh_len, first_slot):
    slot_count = cache.shape[1]
    slot_pos = first_slot + jnp.arange(slot_count, dtype=jnp.int32)
    offsets = slot_pos[None, :] - cached_len[:, None]
    is_live = (offsets >= 0) & (offsets < fresh_len[:, None])
    source_rows = jnp.arange(REQUESTS, dtype=jnp.int32)[:, None] * NEW_TOKENS + jnp.clip(offsets, 0, NEW_TOKENS - 1)
    return jnp.where(is_live[:, :, None], jnp.take(new_rows, source_rows, axis=0), cache)

def reference(hidden, norm_gain, qkv_weight, qkv_bias, out_weight, key_cache, value_cache, cached_len, fresh_len):
    token_count = hidden.shape[0]
    capacity = key_cache.shape[1]
    scale = HEAD_DIM ** (-0.5)
    hidden_f = hidden.astype(jnp.float32)
    mean_square = lax.optimization_barrier(jnp.mean(hidden_f * hidden_f, axis=1, keepdims=True))
    normed = (hidden_f * lax.rsqrt(mean_square + NORM_EPS) * norm_gain[None, :]).astype(jnp.bfloat16)
    projected = jnp.dot(normed, qkv_weight, preferred_element_type=jnp.float32) + qkv_bias.astype(jnp.float32)[None, :]
    queries, new_keys, new_values = finish_rows(projected, cached_len, fresh_len, 0)
    key_out = append_rows(key_cache, new_keys, cached_len, fresh_len, 0)
    value_out = append_rows(value_cache, new_values, cached_len, fresh_len, 0)
    query_blocks = queries.reshape(REQUESTS, NEW_TOKENS, KV_HEADS, GROUP, HEAD_DIM).transpose(0, 2, 1, 3, 4)
    key_blocks = key_out.reshape(REQUESTS, capacity, KV_HEADS, HEAD_DIM).transpose(0, 2, 1, 3)
    value_blocks = value_out.reshape(REQUESTS, capacity, KV_HEADS, HEAD_DIM).transpose(0, 2, 1, 3)
    slot_pos = jnp.arange(capacity, dtype=jnp.int32)
    query_pos = jnp.arange(NEW_TOKENS, dtype=jnp.int32)

    def one_request(items):
        query_req, key_req, value_req, cached_here, fresh_here = items
        visible = (slot_pos[None, :] < cached_here + fresh_here) & (slot_pos[None, :] <= cached_here + query_pos[:, None])

        def one_head(head_items):
            query_head, key_head, value_head = head_items
            scores = jnp.einsum('igd,pd->gip', query_head.astype(jnp.float32), key_head.astype(jnp.float32)) * scale
            scores = jnp.where(visible[None], scores, NEG_LARGE)
            highest = lax.optimization_barrier(jnp.max(scores, axis=2, keepdims=True))
            weighted = jnp.where(visible[None], jnp.exp(scores - highest), 0.0)
            denom = lax.optimization_barrier(jnp.sum(weighted, axis=2))
            rounded = lax.optimization_barrier(weighted.astype(jnp.bfloat16))
            mixed = jnp.einsum('gip,pd->igd', rounded.astype(jnp.float32), value_head.astype(jnp.float32))
            return mixed / denom.T[:, :, None]
        return lax.map(one_head, (query_req, key_req, value_req))
    heads_out = lax.map(one_request, (query_blocks, key_blocks, value_blocks, cached_len, fresh_len))
    heads_out = heads_out.transpose(0, 2, 1, 3, 4).reshape(token_count, HEADS * HEAD_DIM)
    unused_pos, is_live = token_positions(cached_len, fresh_len, 0, token_count)
    attended = jnp.where(is_live[:, None], heads_out, 0.0).astype(jnp.bfloat16)
    projected_out = jnp.dot(attended, out_weight, preferred_element_type=jnp.float32)
    output = (hidden_f + projected_out).astype(jnp.bfloat16)
    return (output, key_out, value_out)
```

```python
import jax
import jax.numpy as jnp
from jax import lax
from jax.sharding import Mesh
from jax.sharding import PartitionSpec as P

HEAD_DIM = 128
GROUP = 5
REQUESTS = 5
NEW_TOKENS = 448


ROPE_THETA = 1000000.0
NORM_EPS = 1e-06
NEG_LARGE = -1e30


def rotate(vectors, positions):
    half_dim = vectors.shape[-1] // 2
    exponent = jnp.arange(half_dim, dtype=jnp.int32).astype(jnp.float32) * (2.0 / vectors.shape[-1])
    frequency = 1.0 / ROPE_THETA**exponent
    angles = positions[:, None] * frequency[None, :]
    target = (positions.shape[0],) + (1,) * (vectors.ndim - 2) + (half_dim,)
    cos_table = jnp.cos(angles).reshape(target)
    sin_table = jnp.sin(angles).reshape(target)
    first_half = vectors[..., :half_dim]
    second_half = vectors[..., half_dim:]
    return jnp.concatenate(
        [
            first_half * cos_table - second_half * sin_table,
            second_half * cos_table + first_half * sin_table,
        ],
        -1,
    )


def token_positions(cached_len, fresh_len, first_row, row_count):
    rows_here = first_row + jnp.arange(row_count, dtype=jnp.int32)
    request = rows_here // NEW_TOKENS
    within = rows_here % NEW_TOKENS
    picked = request[:, None] == jnp.arange(REQUESTS, dtype=jnp.int32)[None, :]
    start_pos = jnp.sum(jnp.where(picked, cached_len[None, :], 0), 1)
    live_count = jnp.sum(jnp.where(picked, fresh_len[None, :], 0), 1)
    return (start_pos + within, within < live_count)


def finish_rows(projected, cached_len, fresh_len, first_row):
    row_count = projected.shape[0]
    groups_here = projected.shape[1] // ((GROUP + 2) * HEAD_DIM)
    shaped = projected.reshape(row_count, groups_here, GROUP + 2, HEAD_DIM)
    positions, unused_live = token_positions(cached_len, fresh_len, first_row, row_count)
    angle_pos = positions.astype(jnp.float32)
    queries = rotate(shaped[:, :, :GROUP], angle_pos).astype(jnp.bfloat16).reshape(row_count, -1)
    new_keys = rotate(shaped[:, :, GROUP], angle_pos).astype(jnp.bfloat16).reshape(row_count, -1)
    new_values = shaped[:, :, GROUP + 1].astype(jnp.bfloat16).reshape(row_count, -1)
    return (queries, new_keys, new_values)


def append_rows(cache, new_rows, cached_len, fresh_len, first_slot):
    slot_count = cache.shape[1]
    slot_pos = first_slot + jnp.arange(slot_count, dtype=jnp.int32)
    offsets = slot_pos[None, :] - cached_len[:, None]
    is_live = (offsets >= 0) & (offsets < fresh_len[:, None])
    source_rows = jnp.arange(REQUESTS, dtype=jnp.int32)[:, None] * NEW_TOKENS + jnp.clip(
        offsets, 0, NEW_TOKENS - 1
    )
    return jnp.where(is_live[:, :, None], jnp.take(new_rows, source_rows, axis=0), cache)


GX = ("y", "zl", "x")
GY = ("zh", "c")


def gather_gx(value):
    for axis in GX[::-1]:
        value = lax.all_gather(value, axis, axis=0, tiled=True)
    return value


def psum_gx(value):
    for axis in GX[::-1]:
        value = lax.psum(value, axis)
    return value


def pmax_gx(value):
    for axis in GX[::-1]:
        value = lax.pmax(value, axis)
    return value


def share_rows(share_sum, cached_len, fresh_len, first_row):
    queries, new_keys, new_values = finish_rows(share_sum, cached_len, fresh_len, first_row)
    widths = (queries.shape[1], new_keys.shape[1])
    joined = gather_gx(jnp.concatenate([queries, new_keys, new_values], axis=1))
    return (
        joined[:, : widths[0]],
        joined[:, widths[0] : widths[0] + widths[1]],
        joined[:, widths[0] + widths[1] :],
    )


def per_device(
    hidden,
    norm_gain,
    qkv_weight,
    qkv_bias,
    out_weight,
    key_cache,
    value_cache,
    cached_len,
    fresh_len,
):
    scale = HEAD_DIM ** (-0.5)
    token_count = REQUESTS * NEW_TOKENS
    gx_size = lax.psum(1, GX)
    model_width = hidden.shape[1] * gx_size
    hidden_f = hidden.astype(jnp.float32)
    squares = psum_gx(jnp.sum(hidden_f * hidden_f, axis=1))
    normed = (
        hidden_f * lax.rsqrt(squares / model_width + NORM_EPS)[:, None] * norm_gain[None, :]
    ).astype(jnp.bfloat16)
    gathered = lax.all_gather(normed, GY, axis=0, tiled=True)
    bias_f = qkv_bias.astype(jnp.float32)[None, :]
    row_share = token_count // gx_size
    share_start = lax.axis_index(GX) * row_share
    summed = lax.psum_scatter(
        jnp.dot(gathered, qkv_weight, preferred_element_type=jnp.float32),
        GX,
        scatter_dimension=0,
        tiled=True,
    )
    queries, new_keys, new_values = share_rows(summed + bias_f, cached_len, fresh_len, share_start)
    slot_count = key_cache.shape[1]
    first_slot = lax.axis_index(GX) * slot_count
    key_out = append_rows(key_cache, new_keys, cached_len, fresh_len, first_slot)
    value_out = append_rows(value_cache, new_values, cached_len, fresh_len, first_slot)
    groups_here = key_cache.shape[2] // HEAD_DIM
    query_blocks = queries.reshape(REQUESTS, NEW_TOKENS, groups_here, GROUP, HEAD_DIM)
    key_blocks = key_out.reshape(REQUESTS, slot_count, groups_here, HEAD_DIM)
    value_blocks = value_out.reshape(REQUESTS, slot_count, groups_here, HEAD_DIM)
    slot_pos = first_slot + jnp.arange(slot_count, dtype=jnp.int32)
    query_pos = jnp.arange(NEW_TOKENS, dtype=jnp.int32)

    def visible_for(cached_here, fresh_here):
        return (slot_pos[None, :] < cached_here + fresh_here) & (
            slot_pos[None, :] <= cached_here + query_pos[:, None]
        )

    def scores_for(query_req, key_req, visible):
        scores = (
            jnp.einsum("ikgd,pkd->kgip", query_req, key_req, preferred_element_type=jnp.float32)
            * scale
        )
        return jnp.where(visible[None, None], scores, NEG_LARGE)

    def local_top(items):
        query_req, key_req, cached_here, fresh_here = items
        return jnp.max(scores_for(query_req, key_req, visible_for(cached_here, fresh_here)), axis=3)

    highest = lax.map(local_top, (query_blocks, key_blocks, cached_len, fresh_len))
    highest = pmax_gx(highest.astype(jnp.bfloat16)).astype(highest.dtype)

    def local_sums(items):
        query_req, key_req, value_req, cached_here, fresh_here, top_here = items
        visible = visible_for(cached_here, fresh_here)
        scores = scores_for(query_req, key_req, visible)
        weighted = jnp.where(visible[None, None], jnp.exp(scores - top_here[..., None]), 0.0)
        denom = jnp.sum(weighted, axis=3)
        mixed = jnp.einsum(
            "kgip,pkd->ikgd",
            weighted.astype(jnp.bfloat16),
            value_req,
            preferred_element_type=jnp.float32,
        )
        return (mixed.reshape(NEW_TOKENS, -1), denom.reshape(-1, NEW_TOKENS).T)

    mixed, denom = lax.map(
        local_sums, (query_blocks, key_blocks, value_blocks, cached_len, fresh_len, highest)
    )
    mixed = mixed.reshape(token_count, -1)
    denom = denom.reshape(token_count, -1)
    mixed_width = mixed.shape[1]
    pad = jnp.zeros((token_count, HEAD_DIM - denom.shape[1]), jnp.float32)
    both = jnp.concatenate([mixed, denom, pad], axis=1).astype(jnp.bfloat16)
    both = lax.psum_scatter(both, GX, scatter_dimension=0, tiled=True).astype(jnp.float32)
    mixed = both[:, :mixed_width]
    denom = both[:, mixed_width : mixed_width + denom.shape[1]]
    unused_pos, is_live = token_positions(cached_len, fresh_len, share_start, row_share)
    ratio = mixed.reshape(row_share, -1, HEAD_DIM) / denom[:, :, None]
    attended = jnp.where(is_live[:, None], ratio.reshape(row_share, -1), 0.0).astype(jnp.bfloat16)
    partial_out = jnp.dot(
        gather_gx(attended),
        out_weight,
        preferred_element_type=jnp.float32,
    )
    summed_out = lax.psum_scatter(
        partial_out.astype(jnp.bfloat16), GY, scatter_dimension=0, tiled=True
    ).astype(jnp.float32)
    output = (hidden_f + summed_out).astype(jnp.bfloat16)
    return (output, key_out, value_out)


def solution(mesh):
    sub_mesh = Mesh(
        mesh.devices.reshape(4, mesh.shape["gx"] // 16, 4, mesh.shape["gy"] // 2, 2), GX + GY
    )
    in_specs = (
        P(GY, GX),
        P(GX),
        P(GX, GY),
        P(GY),
        P(GY, GX),
        P(None, GX, GY),
        P(None, GX, GY),
        P(),
        P(),
    )
    out_specs = (P(GY, GX), P(None, GX, GY), P(None, GX, GY))
    return jax.shard_map(
        per_device, mesh=sub_mesh, in_specs=in_specs, out_specs=out_specs, check_vma=False
    )
```

```python
import jax
import jax.numpy as jnp
from jax import lax
from jax.sharding import Mesh
from jax.sharding import PartitionSpec as P

HEAD_DIM = 128
GROUP = 5
REQUESTS = 5
NEW_TOKENS = 448


ROPE_THETA = 1000000.0
NORM_EPS = 1e-06
NEG_LARGE = -1e30


def rotate(vectors, positions):
    half_dim = vectors.shape[-1] // 2
    exponent = jnp.arange(half_dim, dtype=jnp.int32).astype(jnp.float32) * (2.0 / vectors.shape[-1])
    frequency = 1.0 / ROPE_THETA**exponent
    angles = positions[:, None] * frequency[None, :]
    target = (positions.shape[0],) + (1,) * (vectors.ndim - 2) + (half_dim,)
    cos_table = jnp.cos(angles).reshape(target)
    sin_table = jnp.sin(angles).reshape(target)
    first_half = vectors[..., :half_dim]
    second_half = vectors[..., half_dim:]
    return jnp.concatenate(
        [
            first_half * cos_table - second_half * sin_table,
            second_half * cos_table + first_half * sin_table,
        ],
        -1,
    )


def token_positions(cached_len, fresh_len, first_row, row_count):
    rows_here = first_row + jnp.arange(row_count, dtype=jnp.int32)
    request = rows_here // NEW_TOKENS
    within = rows_here % NEW_TOKENS
    picked = request[:, None] == jnp.arange(REQUESTS, dtype=jnp.int32)[None, :]
    start_pos = jnp.sum(jnp.where(picked, cached_len[None, :], 0), 1)
    live_count = jnp.sum(jnp.where(picked, fresh_len[None, :], 0), 1)
    return (start_pos + within, within < live_count)


def finish_rows(projected, cached_len, fresh_len, first_row):
    row_count = projected.shape[0]
    groups_here = projected.shape[1] // ((GROUP + 2) * HEAD_DIM)
    shaped = projected.reshape(row_count, groups_here, GROUP + 2, HEAD_DIM)
    positions, unused_live = token_positions(cached_len, fresh_len, first_row, row_count)
    angle_pos = positions.astype(jnp.float32)
    queries = rotate(shaped[:, :, :GROUP], angle_pos).astype(jnp.bfloat16).reshape(row_count, -1)
    new_keys = rotate(shaped[:, :, GROUP], angle_pos).astype(jnp.bfloat16).reshape(row_count, -1)
    new_values = shaped[:, :, GROUP + 1].astype(jnp.bfloat16).reshape(row_count, -1)
    return (queries, new_keys, new_values)


def append_rows(cache, new_rows, cached_len, fresh_len, first_slot):
    slot_count = cache.shape[1]
    slot_pos = first_slot + jnp.arange(slot_count, dtype=jnp.int32)
    offsets = slot_pos[None, :] - cached_len[:, None]
    is_live = (offsets >= 0) & (offsets < fresh_len[:, None])
    source_rows = jnp.arange(REQUESTS, dtype=jnp.int32)[:, None] * NEW_TOKENS + jnp.clip(
        offsets, 0, NEW_TOKENS - 1
    )
    return jnp.where(is_live[:, :, None], jnp.take(new_rows, source_rows, axis=0), cache)


GX = ("y", "zl", "x")
GY = ("zh", "c")


def gather_gx(value):
    for axis in GX[::-1]:
        value = lax.all_gather(value, axis, axis=0, tiled=True)
    return value


def psum_gx(value):
    for axis in GX[::-1]:
        value = lax.psum(value, axis)
    return value


def pmax_gx(value):
    for axis in GX[::-1]:
        value = lax.pmax(value, axis)
    return value


def share_rows(share_sum, cached_len, fresh_len, first_row):
    queries, new_keys, new_values = finish_rows(share_sum, cached_len, fresh_len, first_row)
    widths = (queries.shape[1], new_keys.shape[1])
    joined = gather_gx(jnp.concatenate([queries, new_keys, new_values], axis=1))
    return (
        joined[:, : widths[0]],
        joined[:, widths[0] : widths[0] + widths[1]],
        joined[:, widths[0] + widths[1] :],
    )


def per_device(
    hidden,
    norm_gain,
    qkv_weight,
    qkv_bias,
    out_weight,
    key_cache,
    value_cache,
    cached_len,
    fresh_len,
):
    scale = HEAD_DIM ** (-0.5)
    token_count = REQUESTS * NEW_TOKENS
    gx_size = lax.psum(1, GX)
    model_width = hidden.shape[1] * gx_size
    hidden_f = hidden.astype(jnp.float32)
    squares = psum_gx(jnp.sum(hidden_f * hidden_f, axis=1))
    normed = (
        hidden_f * lax.rsqrt(squares / model_width + NORM_EPS)[:, None] * norm_gain[None, :]
    ).astype(jnp.bfloat16)
    gathered = lax.all_gather(normed, GY, axis=0, tiled=True)
    bias_f = qkv_bias.astype(jnp.float32)[None, :]
    row_share = token_count // gx_size
    share_start = lax.axis_index(GX) * row_share
    summed = lax.psum_scatter(
        jnp.dot(gathered, qkv_weight, preferred_element_type=jnp.float32),
        GX,
        scatter_dimension=0,
        tiled=True,
    )
    queries, new_keys, new_values = share_rows(summed + bias_f, cached_len, fresh_len, share_start)
    slot_count = key_cache.shape[1]
    first_slot = lax.axis_index(GX) * slot_count
    key_out = append_rows(key_cache, new_keys, cached_len, fresh_len, first_slot)
    value_out = append_rows(value_cache, new_values, cached_len, fresh_len, first_slot)
    groups_here = key_cache.shape[2] // HEAD_DIM
    query_blocks = queries.reshape(REQUESTS, NEW_TOKENS, groups_here, GROUP, HEAD_DIM)
    key_blocks = key_out.reshape(REQUESTS, slot_count, groups_here, HEAD_DIM)
    value_blocks = value_out.reshape(REQUESTS, slot_count, groups_here, HEAD_DIM)
    slot_pos = first_slot + jnp.arange(slot_count, dtype=jnp.int32)
    query_pos = jnp.arange(NEW_TOKENS, dtype=jnp.int32)

    def visible_for(cached_here, fresh_here):
        return (slot_pos[None, :] < cached_here + fresh_here) & (
            slot_pos[None, :] <= cached_here + query_pos[:, None]
        )

    def scores_for(query_req, key_req, visible):
        scores = (
            jnp.einsum("ikgd,pkd->kgip", query_req, key_req, preferred_element_type=jnp.float32)
            * scale
        )
        return jnp.where(visible[None, None], scores, NEG_LARGE)

    def local_sums(items):
        query_req, key_req, value_req, cached_here, fresh_here = items
        visible = visible_for(cached_here, fresh_here)
        scores = scores_for(query_req, key_req, visible)
        top = jnp.max(scores, axis=3)
        top_hi = top.astype(jnp.bfloat16)
        top_lo = (top - top_hi.astype(jnp.float32)).astype(jnp.bfloat16)
        top_here = top_hi.astype(jnp.float32) + top_lo.astype(jnp.float32)
        weighted = jnp.where(visible[None, None], jnp.exp(scores - top_here[..., None]), 0.0)
        denom = jnp.sum(weighted, axis=3)
        mixed = jnp.einsum(
            "kgip,pkd->ikgd",
            weighted.astype(jnp.bfloat16),
            value_req,
            preferred_element_type=jnp.float32,
        )
        stats = jnp.concatenate(
            [
                top_hi.astype(jnp.float32).reshape(-1, NEW_TOKENS).T,
                top_lo.astype(jnp.float32).reshape(-1, NEW_TOKENS).T,
                denom.reshape(-1, NEW_TOKENS).T,
            ],
            axis=1,
        )
        return (mixed.reshape(NEW_TOKENS, -1), stats)

    mixed, stats = lax.map(local_sums, (query_blocks, key_blocks, value_blocks, cached_len, fresh_len))
    mixed = mixed.reshape(token_count, -1)
    stats = stats.reshape(token_count, -1)
    mixed_width = mixed.shape[1]
    heads_here = mixed_width // HEAD_DIM
    pad = jnp.zeros((token_count, HEAD_DIM - stats.shape[1]), jnp.float32)
    both = jnp.concatenate([mixed, stats, pad], axis=1).astype(jnp.bfloat16)
    both = lax.all_to_all(both, GX, 0, 0, tiled=True).astype(jnp.float32)
    both = both.reshape(gx_size, row_share, -1)
    parts = both[:, :, :mixed_width].reshape(gx_size, row_share, heads_here, HEAD_DIM)
    part_top = (
        both[:, :, mixed_width : mixed_width + heads_here]
        + both[:, :, mixed_width + heads_here : mixed_width + 2 * heads_here]
    )
    part_denom = both[:, :, mixed_width + 2 * heads_here : mixed_width + 3 * heads_here]
    top_all = jnp.max(part_top, axis=0)
    scale_k = jnp.exp(part_top - top_all[None])
    denom = jnp.sum(part_denom * scale_k, axis=0)
    mixed = jnp.sum(parts * scale_k[..., None], axis=0)
    unused_pos, is_live = token_positions(cached_len, fresh_len, share_start, row_share)
    ratio = mixed / denom[:, :, None]
    attended = jnp.where(is_live[:, None], ratio.reshape(row_share, -1), 0.0).astype(jnp.bfloat16)
    partial_out = jnp.dot(
        gather_gx(attended),
        out_weight,
        preferred_element_type=jnp.float32,
    )
    summed_out = lax.psum_scatter(
        partial_out.astype(jnp.bfloat16), GY, scatter_dimension=0, tiled=True
    ).astype(jnp.float32)
    output = (hidden_f + summed_out).astype(jnp.bfloat16)
    return (output, key_out, value_out)


def solution(mesh):
    sub_mesh = Mesh(
        mesh.devices.reshape(4, mesh.shape["gx"] // 16, 4, mesh.shape["gy"] // 2, 2), GX + GY
    )
    in_specs = (
        P(GY, GX),
        P(GX),
        P(GX, GY),
        P(GY),
        P(GY, GX),
        P(None, GX, GY),
        P(None, GX, GY),
        P(),
        P(),
    )
    out_specs = (P(GY, GX), P(None, GX, GY), P(None, GX, GY))
    return jax.shard_map(
        per_device, mesh=sub_mesh, in_specs=in_specs, out_specs=out_specs, check_vma=False
    )
```

```python
import jax
import jax.numpy as jnp
from jax import lax
from jax.sharding import Mesh
from jax.sharding import PartitionSpec as P

HEAD_DIM = 128
GROUP = 5
REQUESTS = 5
NEW_TOKENS = 448


ROPE_THETA = 1000000.0
NORM_EPS = 1e-06
NEG_LARGE = -1e30


def rotate(vectors, positions):
    half_dim = vectors.shape[-1] // 2
    exponent = jnp.arange(half_dim, dtype=jnp.int32).astype(jnp.float32) * (2.0 / vectors.shape[-1])
    frequency = 1.0 / ROPE_THETA**exponent
    angles = positions[:, None] * frequency[None, :]
    target = (positions.shape[0],) + (1,) * (vectors.ndim - 2) + (half_dim,)
    cos_table = jnp.cos(angles).reshape(target)
    sin_table = jnp.sin(angles).reshape(target)
    first_half = vectors[..., :half_dim]
    second_half = vectors[..., half_dim:]
    return jnp.concatenate(
        [
            first_half * cos_table - second_half * sin_table,
            second_half * cos_table + first_half * sin_table,
        ],
        -1,
    )


def token_positions(cached_len, fresh_len, first_row, row_count):
    rows_here = first_row + jnp.arange(row_count, dtype=jnp.int32)
    request = rows_here // NEW_TOKENS
    within = rows_here % NEW_TOKENS
    picked = request[:, None] == jnp.arange(REQUESTS, dtype=jnp.int32)[None, :]
    start_pos = jnp.sum(jnp.where(picked, cached_len[None, :], 0), 1)
    live_count = jnp.sum(jnp.where(picked, fresh_len[None, :], 0), 1)
    return (start_pos + within, within < live_count)


def finish_rows(projected, cached_len, fresh_len, first_row):
    row_count = projected.shape[0]
    groups_here = projected.shape[1] // ((GROUP + 2) * HEAD_DIM)
    shaped = projected.reshape(row_count, groups_here, GROUP + 2, HEAD_DIM)
    positions, unused_live = token_positions(cached_len, fresh_len, first_row, row_count)
    angle_pos = positions.astype(jnp.float32)
    queries = rotate(shaped[:, :, :GROUP], angle_pos).astype(jnp.bfloat16).reshape(row_count, -1)
    new_keys = rotate(shaped[:, :, GROUP], angle_pos).astype(jnp.bfloat16).reshape(row_count, -1)
    new_values = shaped[:, :, GROUP + 1].astype(jnp.bfloat16).reshape(row_count, -1)
    return (queries, new_keys, new_values)


def append_rows(cache, new_rows, cached_len, fresh_len, first_slot):
    slot_count = cache.shape[1]
    slot_pos = first_slot + jnp.arange(slot_count, dtype=jnp.int32)
    offsets = slot_pos[None, :] - cached_len[:, None]
    is_live = (offsets >= 0) & (offsets < fresh_len[:, None])
    source_rows = jnp.arange(REQUESTS, dtype=jnp.int32)[:, None] * NEW_TOKENS + jnp.clip(
        offsets, 0, NEW_TOKENS - 1
    )
    return jnp.where(is_live[:, :, None], jnp.take(new_rows, source_rows, axis=0), cache)


GX = ("y", "zl", "x")
GY = ("zh", "c")


def gather_gx(value):
    for axis in GX[::-1]:
        value = lax.all_gather(value, axis, axis=0, tiled=True)
    return value


def psum_gx(value):
    for axis in GX[::-1]:
        value = lax.psum(value, axis)
    return value


def pmax_gx(value):
    for axis in GX[::-1]:
        value = lax.pmax(value, axis)
    return value


def share_rows(share_sum, cached_len, fresh_len, first_row):
    queries, new_keys, new_values = finish_rows(share_sum, cached_len, fresh_len, first_row)
    widths = (queries.shape[1], new_keys.shape[1])
    joined = gather_gx(jnp.concatenate([queries, new_keys, new_values], axis=1))
    return (
        joined[:, : widths[0]],
        joined[:, widths[0] : widths[0] + widths[1]],
        joined[:, widths[0] + widths[1] :],
    )


def per_device(
    hidden,
    norm_gain,
    qkv_weight,
    qkv_bias,
    out_weight,
    key_cache,
    value_cache,
    cached_len,
    fresh_len,
):
    scale = HEAD_DIM ** (-0.5)
    token_count = REQUESTS * NEW_TOKENS
    gx_size = lax.psum(1, GX)
    model_width = hidden.shape[1] * gx_size
    hidden_f = hidden.astype(jnp.float32)
    gathered = lax.all_gather(hidden, GY, axis=0, tiled=True).astype(jnp.float32)
    squares = jnp.sum(gathered * gathered, axis=1, keepdims=True)
    gained = (gathered * norm_gain[None, :]).astype(jnp.bfloat16)
    bias_f = qkv_bias.astype(jnp.float32)[None, :]
    row_share = token_count // gx_size
    share_start = lax.axis_index(GX) * row_share
    partial = jnp.dot(gained, qkv_weight, preferred_element_type=jnp.float32)
    proj_width = partial.shape[1]
    pad = jnp.zeros((token_count, HEAD_DIM - 1), jnp.float32)
    payload = jnp.concatenate([partial, squares, pad], axis=1).astype(jnp.bfloat16)
    payload = lax.all_to_all(payload, GX, 0, 0, tiled=True).astype(jnp.float32)
    payload = jnp.sum(payload.reshape(gx_size, row_share, -1), axis=0)
    scale_row = lax.rsqrt(payload[:, proj_width : proj_width + 1] / model_width + NORM_EPS)
    summed = payload[:, :proj_width] * scale_row
    queries, new_keys, new_values = share_rows(summed + bias_f, cached_len, fresh_len, share_start)
    slot_count = key_cache.shape[1]
    first_slot = lax.axis_index(GX) * slot_count
    key_out = append_rows(key_cache, new_keys, cached_len, fresh_len, first_slot)
    value_out = append_rows(value_cache, new_values, cached_len, fresh_len, first_slot)
    groups_here = key_cache.shape[2] // HEAD_DIM
    query_blocks = queries.reshape(REQUESTS, NEW_TOKENS, groups_here, GROUP, HEAD_DIM)
    key_blocks = key_out.reshape(REQUESTS, slot_count, groups_here, HEAD_DIM)
    value_blocks = value_out.reshape(REQUESTS, slot_count, groups_here, HEAD_DIM)
    slot_pos = first_slot + jnp.arange(slot_count, dtype=jnp.int32)
    query_pos = jnp.arange(NEW_TOKENS, dtype=jnp.int32)

    def visible_for(cached_here, fresh_here):
        return (slot_pos[None, :] < cached_here + fresh_here) & (
            slot_pos[None, :] <= cached_here + query_pos[:, None]
        )

    def scores_for(query_req, key_req, visible):
        scores = (
            jnp.einsum("ikgd,pkd->kgip", query_req, key_req, preferred_element_type=jnp.float32)
            * scale
        )
        return jnp.where(visible[None, None], scores, NEG_LARGE)

    def local_sums(items):
        query_req, key_req, value_req, cached_here, fresh_here = items
        visible = visible_for(cached_here, fresh_here)
        scores = scores_for(query_req, key_req, visible)
        top = jnp.max(scores, axis=3)
        top_hi = top.astype(jnp.bfloat16)
        top_lo = (top - top_hi.astype(jnp.float32)).astype(jnp.bfloat16)
        top_here = top_hi.astype(jnp.float32) + top_lo.astype(jnp.float32)
        weighted = jnp.where(visible[None, None], jnp.exp(scores - top_here[..., None]), 0.0)
        denom = jnp.sum(weighted, axis=3)
        mixed = jnp.einsum(
            "kgip,pkd->ikgd",
            weighted.astype(jnp.bfloat16),
            value_req,
            preferred_element_type=jnp.float32,
        )
        stats = jnp.concatenate(
            [
                top_hi.astype(jnp.float32).reshape(-1, NEW_TOKENS).T,
                top_lo.astype(jnp.float32).reshape(-1, NEW_TOKENS).T,
                denom.reshape(-1, NEW_TOKENS).T,
            ],
            axis=1,
        )
        return (mixed.reshape(NEW_TOKENS, -1), stats)

    mixed, stats = lax.map(local_sums, (query_blocks, key_blocks, value_blocks, cached_len, fresh_len))
    mixed = mixed.reshape(token_count, -1)
    stats = stats.reshape(token_count, -1)
    mixed_width = mixed.shape[1]
    heads_here = mixed_width // HEAD_DIM
    pad = jnp.zeros((token_count, HEAD_DIM - stats.shape[1]), jnp.float32)
    both = jnp.concatenate([mixed, stats, pad], axis=1).astype(jnp.bfloat16)
    both = lax.all_to_all(both, GX, 0, 0, tiled=True).astype(jnp.float32)
    both = both.reshape(gx_size, row_share, -1)
    parts = both[:, :, :mixed_width].reshape(gx_size, row_share, heads_here, HEAD_DIM)
    part_top = (
        both[:, :, mixed_width : mixed_width + heads_here]
        + both[:, :, mixed_width + heads_here : mixed_width + 2 * heads_here]
    )
    part_denom = both[:, :, mixed_width + 2 * heads_here : mixed_width + 3 * heads_here]
    top_all = jnp.max(part_top, axis=0)
    scale_k = jnp.exp(part_top - top_all[None])
    denom = jnp.sum(part_denom * scale_k, axis=0)
    mixed = jnp.sum(parts * scale_k[..., None], axis=0)
    unused_pos, is_live = token_positions(cached_len, fresh_len, share_start, row_share)
    ratio = mixed / denom[:, :, None]
    attended = jnp.where(is_live[:, None], ratio.reshape(row_share, -1), 0.0).astype(jnp.bfloat16)
    partial_out = jnp.dot(
        gather_gx(attended),
        out_weight,
        preferred_element_type=jnp.float32,
    )
    summed_out = lax.psum_scatter(
        partial_out.astype(jnp.bfloat16), GY, scatter_dimension=0, tiled=True
    ).astype(jnp.float32)
    output = (hidden_f + summed_out).astype(jnp.bfloat16)
    return (output, key_out, value_out)


def solution(mesh):
    sub_mesh = Mesh(
        mesh.devices.reshape(4, mesh.shape["gx"] // 16, 4, mesh.shape["gy"] // 2, 2), GX + GY
    )
    in_specs = (
        P(GY, GX),
        P(GX),
        P(GX, GY),
        P(GY),
        P(GY, GX),
        P(None, GX, GY),
        P(None, GX, GY),
        P(),
        P(),
    )
    out_specs = (P(GY, GX), P(None, GX, GY), P(None, GX, GY))
    return jax.shard_map(
        per_device, mesh=sub_mesh, in_specs=in_specs, out_specs=out_specs, check_vma=False
    )
```

```python
import jax
import jax.numpy as jnp
from jax import lax
from jax.sharding import Mesh
from jax.sharding import PartitionSpec as P

HEAD_DIM = 128
GROUP = 5
REQUESTS = 5
NEW_TOKENS = 448


ROPE_THETA = 1000000.0
NORM_EPS = 1e-06
NEG_LARGE = -1e30


def rotate(vectors, positions):
    half_dim = vectors.shape[-1] // 2
    exponent = jnp.arange(half_dim, dtype=jnp.int32).astype(jnp.float32) * (2.0 / vectors.shape[-1])
    frequency = 1.0 / ROPE_THETA**exponent
    angles = positions[:, None] * frequency[None, :]
    target = (positions.shape[0],) + (1,) * (vectors.ndim - 2) + (half_dim,)
    cos_table = jnp.cos(angles).reshape(target)
    sin_table = jnp.sin(angles).reshape(target)
    first_half = vectors[..., :half_dim]
    second_half = vectors[..., half_dim:]
    return jnp.concatenate(
        [
            first_half * cos_table - second_half * sin_table,
            second_half * cos_table + first_half * sin_table,
        ],
        -1,
    )


def token_positions(cached_len, fresh_len, first_row, row_count):
    rows_here = first_row + jnp.arange(row_count, dtype=jnp.int32)
    request = rows_here // NEW_TOKENS
    within = rows_here % NEW_TOKENS
    picked = request[:, None] == jnp.arange(REQUESTS, dtype=jnp.int32)[None, :]
    start_pos = jnp.sum(jnp.where(picked, cached_len[None, :], 0), 1)
    live_count = jnp.sum(jnp.where(picked, fresh_len[None, :], 0), 1)
    return (start_pos + within, within < live_count)


def finish_rows(projected, cached_len, fresh_len, first_row):
    row_count = projected.shape[0]
    groups_here = projected.shape[1] // ((GROUP + 2) * HEAD_DIM)
    shaped = projected.reshape(row_count, groups_here, GROUP + 2, HEAD_DIM)
    positions, unused_live = token_positions(cached_len, fresh_len, first_row, row_count)
    angle_pos = positions.astype(jnp.float32)
    queries = rotate(shaped[:, :, :GROUP], angle_pos).astype(jnp.bfloat16).reshape(row_count, -1)
    new_keys = rotate(shaped[:, :, GROUP], angle_pos).astype(jnp.bfloat16).reshape(row_count, -1)
    new_values = shaped[:, :, GROUP + 1].astype(jnp.bfloat16).reshape(row_count, -1)
    return (queries, new_keys, new_values)


def append_rows(cache, new_rows, cached_len, fresh_len, first_slot):
    slot_count = cache.shape[1]
    slot_pos = first_slot + jnp.arange(slot_count, dtype=jnp.int32)
    offsets = slot_pos[None, :] - cached_len[:, None]
    is_live = (offsets >= 0) & (offsets < fresh_len[:, None])
    source_rows = jnp.arange(REQUESTS, dtype=jnp.int32)[:, None] * NEW_TOKENS + jnp.clip(
        offsets, 0, NEW_TOKENS - 1
    )
    return jnp.where(is_live[:, :, None], jnp.take(new_rows, source_rows, axis=0), cache)


GX = ("y", "zl", "x")
GY = ("zh", "c")


def gather_gx(value):
    for axis in GX[::-1]:
        value = lax.all_gather(value, axis, axis=0, tiled=True)
    return value


def psum_gx(value):
    for axis in GX[::-1]:
        value = lax.psum(value, axis)
    return value


def pmax_gx(value):
    for axis in GX[::-1]:
        value = lax.pmax(value, axis)
    return value


def share_rows(share_sum, cached_len, fresh_len, first_row):
    queries, new_keys, new_values = finish_rows(share_sum, cached_len, fresh_len, first_row)
    widths = (queries.shape[1], new_keys.shape[1])
    joined = gather_gx(jnp.concatenate([queries, new_keys, new_values], axis=1))
    return (
        joined[:, : widths[0]],
        joined[:, widths[0] : widths[0] + widths[1]],
        joined[:, widths[0] + widths[1] :],
    )


def per_device(
    hidden,
    norm_gain,
    qkv_weight,
    qkv_bias,
    out_weight,
    key_cache,
    value_cache,
    cached_len,
    fresh_len,
):
    scale = HEAD_DIM ** (-0.5)
    token_count = REQUESTS * NEW_TOKENS
    gx_size = lax.psum(1, GX)
    model_width = hidden.shape[1] * gx_size
    hidden_f = hidden.astype(jnp.float32)
    gathered = lax.all_gather(hidden, GY, axis=0, tiled=True).astype(jnp.float32)
    squares = jnp.sum(gathered * gathered, axis=1, keepdims=True)
    gained = (gathered * norm_gain[None, :]).astype(jnp.bfloat16)
    bias_f = qkv_bias.astype(jnp.float32)[None, :]
    row_share = token_count // gx_size
    share_start = lax.axis_index(GX) * row_share
    partial = jnp.dot(gained, qkv_weight, preferred_element_type=jnp.float32)
    proj_width = partial.shape[1]
    pad = jnp.zeros((token_count, HEAD_DIM - 1), jnp.float32)
    payload = jnp.concatenate([partial, squares, pad], axis=1).astype(jnp.bfloat16)
    payload = lax.all_to_all(payload, GX, 0, 0, tiled=True).astype(jnp.float32)
    payload = jnp.sum(payload.reshape(gx_size, row_share, -1), axis=0)
    scale_row = lax.rsqrt(payload[:, proj_width : proj_width + 1] / model_width + NORM_EPS)
    summed = payload[:, :proj_width] * scale_row
    queries, new_keys, new_values = share_rows(summed + bias_f, cached_len, fresh_len, share_start)
    slot_count = key_cache.shape[1]
    first_slot = lax.axis_index(GX) * slot_count
    key_out = append_rows(key_cache, new_keys, cached_len, fresh_len, first_slot)
    value_out = append_rows(value_cache, new_values, cached_len, fresh_len, first_slot)
    groups_here = key_cache.shape[2] // HEAD_DIM
    query_blocks = queries.reshape(REQUESTS, NEW_TOKENS, groups_here, GROUP, HEAD_DIM)
    key_blocks = key_out.reshape(REQUESTS, slot_count, groups_here, HEAD_DIM)
    value_blocks = value_out.reshape(REQUESTS, slot_count, groups_here, HEAD_DIM)
    slot_pos = first_slot + jnp.arange(slot_count, dtype=jnp.int32)
    query_pos = jnp.arange(NEW_TOKENS, dtype=jnp.int32)

    total_len = (cached_len + fresh_len)[:, None, None]
    visible = (slot_pos[None, None, :] < total_len) & (
        slot_pos[None, None, :] <= cached_len[:, None, None] + query_pos[None, :, None]
    )
    scores = (
        jnp.einsum("rikgd,rpkd->rkgip", query_blocks, key_blocks, preferred_element_type=jnp.float32)
        * scale
    )
    scores = jnp.where(visible[:, None, None], scores, NEG_LARGE)
    top = jnp.max(scores, axis=4)
    top_hi = top.astype(jnp.bfloat16)
    top_lo = (top - top_hi.astype(jnp.float32)).astype(jnp.bfloat16)
    top_here = top_hi.astype(jnp.float32) + top_lo.astype(jnp.float32)
    weighted = jnp.where(visible[:, None, None], jnp.exp(scores - top_here[..., None]), 0.0)
    denom = jnp.sum(weighted, axis=4)
    mixed = jnp.einsum(
        "rkgip,rpkd->rikgd",
        weighted.astype(jnp.bfloat16),
        value_blocks,
        preferred_element_type=jnp.float32,
    )

    def per_token(stat):
        return stat.transpose(0, 3, 1, 2).reshape(token_count, -1)

    stats = jnp.concatenate(
        [
            per_token(top_hi.astype(jnp.float32)),
            per_token(top_lo.astype(jnp.float32)),
            per_token(denom),
        ],
        axis=1,
    )
    mixed = mixed.reshape(token_count, -1)
    stats = stats.reshape(token_count, -1)
    mixed_width = mixed.shape[1]
    heads_here = mixed_width // HEAD_DIM
    pad = jnp.zeros((token_count, HEAD_DIM - stats.shape[1]), jnp.float32)
    both = jnp.concatenate([mixed, stats, pad], axis=1).astype(jnp.bfloat16)
    both = lax.all_to_all(both, GX, 0, 0, tiled=True).astype(jnp.float32)
    both = both.reshape(gx_size, row_share, -1)
    parts = both[:, :, :mixed_width].reshape(gx_size, row_share, heads_here, HEAD_DIM)
    part_top = (
        both[:, :, mixed_width : mixed_width + heads_here]
        + both[:, :, mixed_width + heads_here : mixed_width + 2 * heads_here]
    )
    part_denom = both[:, :, mixed_width + 2 * heads_here : mixed_width + 3 * heads_here]
    top_all = jnp.max(part_top, axis=0)
    scale_k = jnp.exp(part_top - top_all[None])
    denom = jnp.sum(part_denom * scale_k, axis=0)
    mixed = jnp.sum(parts * scale_k[..., None], axis=0)
    unused_pos, is_live = token_positions(cached_len, fresh_len, share_start, row_share)
    ratio = mixed / denom[:, :, None]
    attended = jnp.where(is_live[:, None], ratio.reshape(row_share, -1), 0.0).astype(jnp.bfloat16)
    partial_out = jnp.dot(
        gather_gx(attended),
        out_weight,
        preferred_element_type=jnp.float32,
    )
    gy_size = lax.psum(1, GY)
    summed_out = lax.all_to_all(partial_out.astype(jnp.bfloat16), GY, 0, 0, tiled=True)
    summed_out = jnp.sum(summed_out.astype(jnp.float32).reshape(gy_size, token_count // gy_size, -1), axis=0)
    output = (hidden_f + summed_out).astype(jnp.bfloat16)
    return (output, key_out, value_out)


def solution(mesh):
    sub_mesh = Mesh(
        mesh.devices.reshape(4, mesh.shape["gx"] // 16, 4, mesh.shape["gy"] // 2, 2), GX + GY
    )
    in_specs = (
        P(GY, GX),
        P(GX),
        P(GX, GY),
        P(GY),
        P(GY, GX),
        P(None, GX, GY),
        P(None, GX, GY),
        P(),
        P(),
    )
    out_specs = (P(GY, GX), P(None, GX, GY), P(None, GX, GY))
    return jax.shard_map(
        per_device, mesh=sub_mesh, in_specs=in_specs, out_specs=out_specs, check_vma=False
    )
```

```python
import jax
import jax.numpy as jnp
from jax import lax
from jax.sharding import Mesh
from jax.sharding import PartitionSpec as P

HEAD_DIM = 128
GROUP = 5
REQUESTS = 5
NEW_TOKENS = 448


ROPE_THETA = 1000000.0
NORM_EPS = 1e-06
NEG_LARGE = -1e30


def rotate(vectors, positions):
    half_dim = vectors.shape[-1] // 2
    exponent = jnp.arange(half_dim, dtype=jnp.int32).astype(jnp.float32) * (2.0 / vectors.shape[-1])
    frequency = 1.0 / ROPE_THETA**exponent
    angles = positions[:, None] * frequency[None, :]
    target = (positions.shape[0],) + (1,) * (vectors.ndim - 2) + (half_dim,)
    cos_table = jnp.cos(angles).reshape(target)
    sin_table = jnp.sin(angles).reshape(target)
    first_half = vectors[..., :half_dim]
    second_half = vectors[..., half_dim:]
    return jnp.concatenate(
        [
            first_half * cos_table - second_half * sin_table,
            second_half * cos_table + first_half * sin_table,
        ],
        -1,
    )


def token_positions(cached_len, fresh_len, first_row, row_count):
    rows_here = first_row + jnp.arange(row_count, dtype=jnp.int32)
    request = rows_here // NEW_TOKENS
    within = rows_here % NEW_TOKENS
    picked = request[:, None] == jnp.arange(REQUESTS, dtype=jnp.int32)[None, :]
    start_pos = jnp.sum(jnp.where(picked, cached_len[None, :], 0), 1)
    live_count = jnp.sum(jnp.where(picked, fresh_len[None, :], 0), 1)
    return (start_pos + within, within < live_count)


def finish_rows(projected, cached_len, fresh_len, first_row):
    row_count = projected.shape[0]
    groups_here = projected.shape[1] // ((GROUP + 2) * HEAD_DIM)
    shaped = projected.reshape(row_count, groups_here, GROUP + 2, HEAD_DIM)
    positions, unused_live = token_positions(cached_len, fresh_len, first_row, row_count)
    angle_pos = positions.astype(jnp.float32)
    queries = rotate(shaped[:, :, :GROUP], angle_pos).astype(jnp.bfloat16).reshape(row_count, -1)
    new_keys = rotate(shaped[:, :, GROUP], angle_pos).astype(jnp.bfloat16).reshape(row_count, -1)
    new_values = shaped[:, :, GROUP + 1].astype(jnp.bfloat16).reshape(row_count, -1)
    return (queries, new_keys, new_values)


def append_rows(cache, new_rows, cached_len, fresh_len, first_slot):
    slot_count = cache.shape[1]
    slot_pos = first_slot + jnp.arange(slot_count, dtype=jnp.int32)
    offsets = slot_pos[None, :] - cached_len[:, None]
    is_live = (offsets >= 0) & (offsets < fresh_len[:, None])
    source_rows = jnp.arange(REQUESTS, dtype=jnp.int32)[:, None] * NEW_TOKENS + jnp.clip(
        offsets, 0, NEW_TOKENS - 1
    )
    return jnp.where(is_live[:, :, None], jnp.take(new_rows, source_rows, axis=0), cache)


GX = ("y", "zl", "x")
GY = ("zh", "c")


def gather_gx(value):
    for axis in GX[::-1]:
        value = lax.all_gather(value, axis, axis=0, tiled=True)
    return value


def psum_gx(value):
    for axis in GX[::-1]:
        value = lax.psum(value, axis)
    return value


def pmax_gx(value):
    for axis in GX[::-1]:
        value = lax.pmax(value, axis)
    return value


def share_rows(share_sum, cached_len, fresh_len, first_row):
    queries, new_keys, new_values = finish_rows(share_sum, cached_len, fresh_len, first_row)
    widths = (queries.shape[1], new_keys.shape[1])
    joined = gather_gx(jnp.concatenate([queries, new_keys, new_values], axis=1))
    return (
        joined[:, : widths[0]],
        joined[:, widths[0] : widths[0] + widths[1]],
        joined[:, widths[0] + widths[1] :],
    )


def per_device(
    hidden,
    norm_gain,
    qkv_weight,
    qkv_bias,
    out_weight,
    key_cache,
    value_cache,
    cached_len,
    fresh_len,
):
    scale = HEAD_DIM ** (-0.5)
    token_count = REQUESTS * NEW_TOKENS
    gx_size = lax.psum(1, GX)
    model_width = hidden.shape[1] * gx_size
    hidden_f = hidden.astype(jnp.float32)
    gathered = lax.all_gather(hidden, GY, axis=0, tiled=True).astype(jnp.float32)
    squares = jnp.sum(gathered * gathered, axis=1, keepdims=True)
    gained = (gathered * norm_gain[None, :]).astype(jnp.bfloat16)
    bias_f = qkv_bias.astype(jnp.float32)[None, :]
    row_share = token_count // gx_size
    share_start = lax.axis_index(GX) * row_share
    partial = jnp.dot(gained, qkv_weight, preferred_element_type=jnp.float32)
    proj_width = partial.shape[1]
    pad = jnp.zeros((token_count, HEAD_DIM - 1), jnp.bfloat16)
    payload = jnp.concatenate(
        [partial.astype(jnp.bfloat16), squares.astype(jnp.bfloat16), pad], axis=1
    )
    payload = lax.all_to_all(payload, GX, 0, 0, tiled=True).astype(jnp.float32)
    payload = jnp.sum(payload.reshape(gx_size, row_share, -1), axis=0)
    scale_row = lax.rsqrt(payload[:, proj_width : proj_width + 1] / model_width + NORM_EPS)
    summed = payload[:, :proj_width] * scale_row
    queries, new_keys, new_values = share_rows(summed + bias_f, cached_len, fresh_len, share_start)
    slot_count = key_cache.shape[1]
    first_slot = lax.axis_index(GX) * slot_count
    key_out = append_rows(key_cache, new_keys, cached_len, fresh_len, first_slot)
    value_out = append_rows(value_cache, new_values, cached_len, fresh_len, first_slot)
    groups_here = key_cache.shape[2] // HEAD_DIM
    query_blocks = queries.reshape(REQUESTS, NEW_TOKENS, groups_here, GROUP, HEAD_DIM)
    key_blocks = key_out.reshape(REQUESTS, slot_count, groups_here, HEAD_DIM)
    value_blocks = value_out.reshape(REQUESTS, slot_count, groups_here, HEAD_DIM)
    slot_pos = first_slot + jnp.arange(slot_count, dtype=jnp.int32)
    query_pos = jnp.arange(NEW_TOKENS, dtype=jnp.int32)

    total_len = (cached_len + fresh_len)[:, None, None]
    visible = (slot_pos[None, None, :] < total_len) & (
        slot_pos[None, None, :] <= cached_len[:, None, None] + query_pos[None, :, None]
    )
    scores = (
        jnp.einsum("rikgd,rpkd->rkgip", query_blocks, key_blocks, preferred_element_type=jnp.float32)
        * scale
    )
    scores = jnp.where(visible[:, None, None], scores, NEG_LARGE)
    top = jnp.max(scores, axis=4)
    top_hi = top.astype(jnp.bfloat16)
    top_lo = (top - top_hi.astype(jnp.float32)).astype(jnp.bfloat16)
    top_here = top_hi.astype(jnp.float32) + top_lo.astype(jnp.float32)
    weighted = jnp.where(visible[:, None, None], jnp.exp(scores - top_here[..., None]), 0.0)
    denom = jnp.sum(weighted, axis=4)
    mixed = jnp.einsum(
        "rkgip,rpkd->rikgd",
        weighted.astype(jnp.bfloat16),
        value_blocks,
        preferred_element_type=jnp.float32,
    )

    def per_token(stat):
        return stat.transpose(0, 3, 1, 2).reshape(token_count, -1)

    stats = jnp.concatenate(
        [
            per_token(top_hi.astype(jnp.float32)),
            per_token(top_lo.astype(jnp.float32)),
            per_token(denom),
        ],
        axis=1,
    )
    mixed = mixed.reshape(token_count, -1)
    stats = stats.reshape(token_count, -1)
    mixed_width = mixed.shape[1]
    heads_here = mixed_width // HEAD_DIM
    pad = jnp.zeros((token_count, HEAD_DIM - stats.shape[1]), jnp.bfloat16)
    both = jnp.concatenate(
        [mixed.astype(jnp.bfloat16), stats.astype(jnp.bfloat16), pad], axis=1
    )
    both = lax.all_to_all(both, GX, 0, 0, tiled=True).astype(jnp.float32)
    both = both.reshape(gx_size, row_share, -1)
    parts = both[:, :, :mixed_width].reshape(gx_size, row_share, heads_here, HEAD_DIM)
    part_top = (
        both[:, :, mixed_width : mixed_width + heads_here]
        + both[:, :, mixed_width + heads_here : mixed_width + 2 * heads_here]
    )
    part_denom = both[:, :, mixed_width + 2 * heads_here : mixed_width + 3 * heads_here]
    top_all = jnp.max(part_top, axis=0)
    scale_k = jnp.exp(part_top - top_all[None])
    denom = jnp.sum(part_denom * scale_k, axis=0)
    mixed = jnp.sum(parts * scale_k[..., None], axis=0)
    unused_pos, is_live = token_positions(cached_len, fresh_len, share_start, row_share)
    ratio = mixed / denom[:, :, None]
    attended = jnp.where(is_live[:, None], ratio.reshape(row_share, -1), 0.0).astype(jnp.bfloat16)
    partial_out = jnp.dot(
        gather_gx(attended),
        out_weight,
        preferred_element_type=jnp.float32,
    )
    gy_size = lax.psum(1, GY)
    summed_out = lax.all_to_all(partial_out.astype(jnp.bfloat16), GY, 0, 0, tiled=True)
    summed_out = jnp.sum(summed_out.astype(jnp.float32).reshape(gy_size, token_count // gy_size, -1), axis=0)
    output = (hidden_f + summed_out).astype(jnp.bfloat16)
    return (output, key_out, value_out)


def solution(mesh):
    sub_mesh = Mesh(
        mesh.devices.reshape(4, mesh.shape["gx"] // 16, 4, mesh.shape["gy"] // 2, 2), GX + GY
    )
    in_specs = (
        P(GY, GX),
        P(GX),
        P(GX, GY),
        P(GY),
        P(GY, GX),
        P(None, GX, GY),
        P(None, GX, GY),
        P(),
        P(),
    )
    out_specs = (P(GY, GX), P(None, GX, GY), P(None, GX, GY))
    return jax.shard_map(
        per_device, mesh=sub_mesh, in_specs=in_specs, out_specs=out_specs, check_vma=False
    )
```

```python
import jax
import jax.numpy as jnp
from jax import lax
from jax.sharding import Mesh
from jax.sharding import PartitionSpec as P

HEAD_DIM = 128
GROUP = 5
REQUESTS = 5
NEW_TOKENS = 448


ROPE_THETA = 1000000.0
NORM_EPS = 1e-06
NEG_LARGE = -1e30


def rotate(vectors, positions):
    half_dim = vectors.shape[-1] // 2
    exponent = jnp.arange(half_dim, dtype=jnp.int32).astype(jnp.float32) * (2.0 / vectors.shape[-1])
    frequency = 1.0 / ROPE_THETA**exponent
    angles = positions[:, None] * frequency[None, :]
    target = (positions.shape[0],) + (1,) * (vectors.ndim - 2) + (half_dim,)
    cos_table = jnp.cos(angles).reshape(target)
    sin_table = jnp.sin(angles).reshape(target)
    first_half = vectors[..., :half_dim]
    second_half = vectors[..., half_dim:]
    return jnp.concatenate(
        [
            first_half * cos_table - second_half * sin_table,
            second_half * cos_table + first_half * sin_table,
        ],
        -1,
    )


def token_positions(cached_len, fresh_len, first_row, row_count):
    rows_here = first_row + jnp.arange(row_count, dtype=jnp.int32)
    request = rows_here // NEW_TOKENS
    within = rows_here % NEW_TOKENS
    picked = request[:, None] == jnp.arange(REQUESTS, dtype=jnp.int32)[None, :]
    start_pos = jnp.sum(jnp.where(picked, cached_len[None, :], 0), 1)
    live_count = jnp.sum(jnp.where(picked, fresh_len[None, :], 0), 1)
    return (start_pos + within, within < live_count)


def finish_rows(projected, cached_len, fresh_len, first_row):
    row_count = projected.shape[0]
    groups_here = projected.shape[1] // ((GROUP + 2) * HEAD_DIM)
    shaped = projected.reshape(row_count, groups_here, GROUP + 2, HEAD_DIM)
    positions, unused_live = token_positions(cached_len, fresh_len, first_row, row_count)
    angle_pos = positions.astype(jnp.float32)
    queries = rotate(shaped[:, :, :GROUP], angle_pos).astype(jnp.bfloat16).reshape(row_count, -1)
    new_keys = rotate(shaped[:, :, GROUP], angle_pos).astype(jnp.bfloat16).reshape(row_count, -1)
    new_values = shaped[:, :, GROUP + 1].astype(jnp.bfloat16).reshape(row_count, -1)
    return (queries, new_keys, new_values)


def append_rows(cache, new_rows, cached_len, fresh_len, first_slot):
    slot_count = cache.shape[1]
    slot_pos = first_slot + jnp.arange(slot_count, dtype=jnp.int32)
    offsets = slot_pos[None, :] - cached_len[:, None]
    is_live = (offsets >= 0) & (offsets < fresh_len[:, None])
    source_rows = jnp.arange(REQUESTS, dtype=jnp.int32)[:, None] * NEW_TOKENS + jnp.clip(
        offsets, 0, NEW_TOKENS - 1
    )
    return jnp.where(is_live[:, :, None], jnp.take(new_rows, source_rows, axis=0), cache)


GX = ("y", "zl", "x")
GY = ("zh", "c")


def gather_gx(value):
    for axis in GX[::-1]:
        value = lax.all_gather(value, axis, axis=0, tiled=True)
    return value


def psum_gx(value):
    for axis in GX[::-1]:
        value = lax.psum(value, axis)
    return value


def pmax_gx(value):
    for axis in GX[::-1]:
        value = lax.pmax(value, axis)
    return value


def share_rows(share_sum, cached_len, fresh_len, first_row):
    queries, new_keys, new_values = finish_rows(share_sum, cached_len, fresh_len, first_row)
    widths = (queries.shape[1], new_keys.shape[1])
    joined = gather_gx(jnp.concatenate([queries, new_keys, new_values], axis=1))
    return (
        joined[:, : widths[0]],
        joined[:, widths[0] : widths[0] + widths[1]],
        joined[:, widths[0] + widths[1] :],
    )


def per_device(
    hidden,
    norm_gain,
    qkv_weight,
    qkv_bias,
    out_weight,
    key_cache,
    value_cache,
    cached_len,
    fresh_len,
):
    scale = HEAD_DIM ** (-0.5)
    token_count = REQUESTS * NEW_TOKENS
    gx_size = lax.psum(1, GX)
    model_width = hidden.shape[1] * gx_size
    hidden_f = hidden.astype(jnp.float32)
    gathered = lax.all_gather(hidden, GY, axis=0, tiled=True).astype(jnp.float32)
    squares = jnp.sum(gathered * gathered, axis=1, keepdims=True)
    gained = (gathered * norm_gain[None, :]).astype(jnp.bfloat16)
    bias_f = qkv_bias.astype(jnp.float32)[None, :]
    row_share = token_count // gx_size
    share_start = lax.axis_index(GX) * row_share
    partial = jnp.dot(gained, qkv_weight, preferred_element_type=jnp.float32)
    proj_width = partial.shape[1]
    pad = jnp.zeros((token_count, HEAD_DIM - 1), jnp.float32)
    payload = jnp.concatenate([partial, squares, pad], axis=1).astype(jnp.bfloat16)
    payload = lax.all_to_all(payload, GX, 0, 0, tiled=True).astype(jnp.float32)
    payload = jnp.sum(payload.reshape(gx_size, row_share, -1), axis=0)
    scale_row = lax.rsqrt(payload[:, proj_width : proj_width + 1] / model_width + NORM_EPS)
    summed = payload[:, :proj_width] * scale_row
    queries, new_keys, new_values = share_rows(summed + bias_f, cached_len, fresh_len, share_start)
    slot_count = key_cache.shape[1]
    first_slot = lax.axis_index(GX) * slot_count
    key_out = append_rows(key_cache, new_keys, cached_len, fresh_len, first_slot)
    value_out = append_rows(value_cache, new_values, cached_len, fresh_len, first_slot)
    groups_here = key_cache.shape[2] // HEAD_DIM
    query_blocks = queries.reshape(REQUESTS, NEW_TOKENS, groups_here, GROUP, HEAD_DIM)
    key_blocks = key_out.reshape(REQUESTS, slot_count, groups_here, HEAD_DIM)
    value_blocks = value_out.reshape(REQUESTS, slot_count, groups_here, HEAD_DIM)
    slot_pos = first_slot + jnp.arange(slot_count, dtype=jnp.int32)
    query_pos = jnp.arange(NEW_TOKENS, dtype=jnp.int32)

    total_len = (cached_len + fresh_len)[:, None, None]
    visible = (slot_pos[None, None, :] < total_len) & (
        slot_pos[None, None, :] <= cached_len[:, None, None] + query_pos[None, :, None]
    )
    scores = (
        jnp.einsum("rikgd,rpkd->rkgip", query_blocks, key_blocks, preferred_element_type=jnp.float32)
        * scale
    )
    scores = jnp.where(visible[:, None, None], scores, NEG_LARGE)
    top = jnp.max(scores, axis=4)
    top_hi = top.astype(jnp.bfloat16)
    top_lo = (top - top_hi.astype(jnp.float32)).astype(jnp.bfloat16)
    top_here = top_hi.astype(jnp.float32) + top_lo.astype(jnp.float32)
    weighted = jnp.where(visible[:, None, None], jnp.exp(scores - top_here[..., None]), 0.0)
    denom = jnp.sum(weighted, axis=4)
    mixed = jnp.einsum(
        "rkgip,rpkd->rikgd",
        weighted.astype(jnp.bfloat16),
        value_blocks,
        preferred_element_type=jnp.float32,
    )

    def per_token(stat):
        return stat.transpose(0, 3, 1, 2).reshape(token_count, -1)

    stats = jnp.concatenate(
        [
            per_token(top_hi.astype(jnp.float32)),
            per_token(top_lo.astype(jnp.float32)),
            per_token(denom),
        ],
        axis=1,
    )
    mixed = mixed.reshape(token_count, -1)
    stats = stats.reshape(token_count, -1)
    mixed_width = mixed.shape[1]
    heads_here = mixed_width // HEAD_DIM
    pad = jnp.zeros((token_count, HEAD_DIM - stats.shape[1]), jnp.float32)
    both = jnp.concatenate([mixed, stats, pad], axis=1).astype(jnp.bfloat16)
    both = lax.all_to_all(both, GX, 0, 0, tiled=True)
    both = both.reshape(gx_size, row_share, -1)
    part_stats = both[:, :, mixed_width : mixed_width + 3 * heads_here].astype(jnp.float32)
    part_top = part_stats[:, :, :heads_here] + part_stats[:, :, heads_here : 2 * heads_here]
    part_denom = part_stats[:, :, 2 * heads_here :]
    top_all = jnp.max(part_top, axis=0)
    scale_k = jnp.exp(part_top - top_all[None])
    denom = jnp.sum(part_denom * scale_k, axis=0)
    weight_k = scale_k / denom[None]
    parts = both[:, :, :mixed_width].reshape(gx_size, row_share, heads_here, HEAD_DIM)
    mixed = jnp.sum(parts.astype(jnp.float32) * weight_k[..., None], axis=0)
    unused_pos, is_live = token_positions(cached_len, fresh_len, share_start, row_share)
    ratio = mixed
    attended = jnp.where(is_live[:, None], ratio.reshape(row_share, -1), 0.0).astype(jnp.bfloat16)
    partial_out = jnp.dot(
        gather_gx(attended),
        out_weight,
        preferred_element_type=jnp.float32,
    )
    gy_size = lax.psum(1, GY)
    summed_out = lax.all_to_all(partial_out.astype(jnp.bfloat16), GY, 0, 0, tiled=True)
    summed_out = jnp.sum(summed_out.astype(jnp.float32).reshape(gy_size, token_count // gy_size, -1), axis=0)
    output = (hidden_f + summed_out).astype(jnp.bfloat16)
    return (output, key_out, value_out)


def solution(mesh):
    sub_mesh = Mesh(
        mesh.devices.reshape(4, mesh.shape["gx"] // 16, 4, mesh.shape["gy"] // 2, 2), GX + GY
    )
    in_specs = (
        P(GY, GX),
        P(GX),
        P(GX, GY),
        P(GY),
        P(GY, GX),
        P(None, GX, GY),
        P(None, GX, GY),
        P(),
        P(),
    )
    out_specs = (P(GY, GX), P(None, GX, GY), P(None, GX, GY))
    return jax.shard_map(
        per_device, mesh=sub_mesh, in_specs=in_specs, out_specs=out_specs, check_vma=False
    )
```

```python
import jax
import jax.numpy as jnp
from jax import lax
from jax.sharding import Mesh
from jax.sharding import PartitionSpec as P

HEAD_DIM = 128
GROUP = 5
REQUESTS = 5
NEW_TOKENS = 448


ROPE_THETA = 1000000.0
NORM_EPS = 1e-06
NEG_LARGE = -1e30


def rotate(vectors, positions):
    half_dim = vectors.shape[-1] // 2
    exponent = jnp.arange(half_dim, dtype=jnp.int32).astype(jnp.float32) * (2.0 / vectors.shape[-1])
    frequency = 1.0 / ROPE_THETA**exponent
    angles = positions[:, None] * frequency[None, :]
    target = (positions.shape[0],) + (1,) * (vectors.ndim - 2) + (half_dim,)
    cos_table = jnp.cos(angles).reshape(target)
    sin_table = jnp.sin(angles).reshape(target)
    first_half = vectors[..., :half_dim]
    second_half = vectors[..., half_dim:]
    return jnp.concatenate(
        [
            first_half * cos_table - second_half * sin_table,
            second_half * cos_table + first_half * sin_table,
        ],
        -1,
    )


def token_positions(cached_len, fresh_len, first_row, row_count):
    rows_here = first_row + jnp.arange(row_count, dtype=jnp.int32)
    request = rows_here // NEW_TOKENS
    within = rows_here % NEW_TOKENS
    picked = request[:, None] == jnp.arange(REQUESTS, dtype=jnp.int32)[None, :]
    start_pos = jnp.sum(jnp.where(picked, cached_len[None, :], 0), 1)
    live_count = jnp.sum(jnp.where(picked, fresh_len[None, :], 0), 1)
    return (start_pos + within, within < live_count)


def finish_rows(projected, cached_len, fresh_len, first_row):
    row_count = projected.shape[0]
    groups_here = projected.shape[1] // ((GROUP + 2) * HEAD_DIM)
    shaped = projected.reshape(row_count, groups_here, GROUP + 2, HEAD_DIM)
    positions, unused_live = token_positions(cached_len, fresh_len, first_row, row_count)
    angle_pos = positions.astype(jnp.float32)
    queries = rotate(shaped[:, :, :GROUP], angle_pos).astype(jnp.bfloat16).reshape(row_count, -1)
    new_keys = rotate(shaped[:, :, GROUP], angle_pos).astype(jnp.bfloat16).reshape(row_count, -1)
    new_values = shaped[:, :, GROUP + 1].astype(jnp.bfloat16).reshape(row_count, -1)
    return (queries, new_keys, new_values)


def append_rows(cache, new_rows, cached_len, fresh_len, first_slot):
    slot_count = cache.shape[1]
    slot_pos = first_slot + jnp.arange(slot_count, dtype=jnp.int32)
    offsets = slot_pos[None, :] - cached_len[:, None]
    is_live = (offsets >= 0) & (offsets < fresh_len[:, None])
    source_rows = jnp.arange(REQUESTS, dtype=jnp.int32)[:, None] * NEW_TOKENS + jnp.clip(
        offsets, 0, NEW_TOKENS - 1
    )
    return jnp.where(is_live[:, :, None], jnp.take(new_rows, source_rows, axis=0), cache)


GX = ("y", "zl", "x")
GY = ("zh", "c")


def gather_gx(value):
    copies = lax.psum(1, GX)
    tiled = jnp.tile(value, (copies,) + (1,) * (value.ndim - 1))
    return lax.all_to_all(tiled, GX, 0, 0, tiled=True)


def psum_gx(value):
    for axis in GX[::-1]:
        value = lax.psum(value, axis)
    return value


def pmax_gx(value):
    for axis in GX[::-1]:
        value = lax.pmax(value, axis)
    return value


def share_rows(share_sum, cached_len, fresh_len, first_row):
    queries, new_keys, new_values = finish_rows(share_sum, cached_len, fresh_len, first_row)
    widths = (queries.shape[1], new_keys.shape[1])
    joined = gather_gx(jnp.concatenate([queries, new_keys, new_values], axis=1))
    return (
        joined[:, : widths[0]],
        joined[:, widths[0] : widths[0] + widths[1]],
        joined[:, widths[0] + widths[1] :],
    )


def per_device(
    hidden,
    norm_gain,
    qkv_weight,
    qkv_bias,
    out_weight,
    key_cache,
    value_cache,
    cached_len,
    fresh_len,
):
    scale = HEAD_DIM ** (-0.5)
    token_count = REQUESTS * NEW_TOKENS
    gx_size = lax.psum(1, GX)
    model_width = hidden.shape[1] * gx_size
    hidden_f = hidden.astype(jnp.float32)
    gathered = lax.all_gather(hidden, GY, axis=0, tiled=True).astype(jnp.float32)
    squares = jnp.sum(gathered * gathered, axis=1, keepdims=True)
    gained = (gathered * norm_gain[None, :]).astype(jnp.bfloat16)
    bias_f = qkv_bias.astype(jnp.float32)[None, :]
    row_share = token_count // gx_size
    share_start = lax.axis_index(GX) * row_share
    partial = jnp.dot(gained, qkv_weight, preferred_element_type=jnp.float32)
    proj_width = partial.shape[1]
    pad = jnp.zeros((token_count, HEAD_DIM - 1), jnp.float32)
    payload = jnp.concatenate([partial, squares, pad], axis=1).astype(jnp.bfloat16)
    payload = lax.all_to_all(payload, GX, 0, 0, tiled=True).astype(jnp.float32)
    payload = jnp.sum(payload.reshape(gx_size, row_share, -1), axis=0)
    scale_row = lax.rsqrt(payload[:, proj_width : proj_width + 1] / model_width + NORM_EPS)
    summed = payload[:, :proj_width] * scale_row
    queries, new_keys, new_values = share_rows(summed + bias_f, cached_len, fresh_len, share_start)
    slot_count = key_cache.shape[1]
    first_slot = lax.axis_index(GX) * slot_count
    key_out = append_rows(key_cache, new_keys, cached_len, fresh_len, first_slot)
    value_out = append_rows(value_cache, new_values, cached_len, fresh_len, first_slot)
    groups_here = key_cache.shape[2] // HEAD_DIM
    query_blocks = queries.reshape(REQUESTS, NEW_TOKENS, groups_here, GROUP, HEAD_DIM)
    key_blocks = key_out.reshape(REQUESTS, slot_count, groups_here, HEAD_DIM)
    value_blocks = value_out.reshape(REQUESTS, slot_count, groups_here, HEAD_DIM)
    slot_pos = first_slot + jnp.arange(slot_count, dtype=jnp.int32)
    query_pos = jnp.arange(NEW_TOKENS, dtype=jnp.int32)

    total_len = (cached_len + fresh_len)[:, None, None]
    visible = (slot_pos[None, None, :] < total_len) & (
        slot_pos[None, None, :] <= cached_len[:, None, None] + query_pos[None, :, None]
    )
    scores = (
        jnp.einsum("rikgd,rpkd->rkgip", query_blocks, key_blocks, preferred_element_type=jnp.float32)
        * scale
    )
    scores = jnp.where(visible[:, None, None], scores, NEG_LARGE)
    top = jnp.max(scores, axis=4)
    top_hi = top.astype(jnp.bfloat16)
    top_lo = (top - top_hi.astype(jnp.float32)).astype(jnp.bfloat16)
    top_here = top_hi.astype(jnp.float32) + top_lo.astype(jnp.float32)
    weighted = jnp.where(visible[:, None, None], jnp.exp(scores - top_here[..., None]), 0.0)
    denom = jnp.sum(weighted, axis=4)
    mixed = jnp.einsum(
        "rkgip,rpkd->rikgd",
        weighted.astype(jnp.bfloat16),
        value_blocks,
        preferred_element_type=jnp.float32,
    )

    def per_token(stat):
        return stat.transpose(0, 3, 1, 2).reshape(token_count, -1)

    stats = jnp.concatenate(
        [
            per_token(top_hi.astype(jnp.float32)),
            per_token(top_lo.astype(jnp.float32)),
            per_token(denom),
        ],
        axis=1,
    )
    mixed = mixed.reshape(token_count, -1)
    stats = stats.reshape(token_count, -1)
    mixed_width = mixed.shape[1]
    heads_here = mixed_width // HEAD_DIM
    pad = jnp.zeros((token_count, HEAD_DIM - stats.shape[1]), jnp.float32)
    both = jnp.concatenate([mixed, stats, pad], axis=1).astype(jnp.bfloat16)
    both = lax.all_to_all(both, GX, 0, 0, tiled=True)
    both = both.reshape(gx_size, row_share, -1)
    part_stats = both[:, :, mixed_width : mixed_width + 3 * heads_here].astype(jnp.float32)
    part_top = part_stats[:, :, :heads_here] + part_stats[:, :, heads_here : 2 * heads_here]
    part_denom = part_stats[:, :, 2 * heads_here :]
    top_all = jnp.max(part_top, axis=0)
    scale_k = jnp.exp(part_top - top_all[None])
    denom = jnp.sum(part_denom * scale_k, axis=0)
    weight_k = scale_k / denom[None]
    parts = both[:, :, :mixed_width].reshape(gx_size, row_share, heads_here, HEAD_DIM)
    mixed = jnp.sum(parts.astype(jnp.float32) * weight_k[..., None], axis=0)
    unused_pos, is_live = token_positions(cached_len, fresh_len, share_start, row_share)
    ratio = mixed
    attended = jnp.where(is_live[:, None], ratio.reshape(row_share, -1), 0.0).astype(jnp.bfloat16)
    partial_out = jnp.dot(
        gather_gx(attended),
        out_weight,
        preferred_element_type=jnp.float32,
    )
    gy_size = lax.psum(1, GY)
    summed_out = lax.all_to_all(partial_out.astype(jnp.bfloat16), GY, 0, 0, tiled=True)
    summed_out = jnp.sum(summed_out.astype(jnp.float32).reshape(gy_size, token_count // gy_size, -1), axis=0)
    output = (hidden_f + summed_out).astype(jnp.bfloat16)
    return (output, key_out, value_out)


def solution(mesh):
    sub_mesh = Mesh(
        mesh.devices.reshape(4, mesh.shape["gx"] // 16, 4, mesh.shape["gy"] // 2, 2), GX + GY
    )
    in_specs = (
        P(GY, GX),
        P(GX),
        P(GX, GY),
        P(GY),
        P(GY, GX),
        P(None, GX, GY),
        P(None, GX, GY),
        P(),
        P(),
    )
    out_specs = (P(GY, GX), P(None, GX, GY), P(None, GX, GY))
    return jax.shard_map(
        per_device, mesh=sub_mesh, in_specs=in_specs, out_specs=out_specs, check_vma=False
    )
```

```python
import jax
import jax.numpy as jnp
from jax import lax
from jax.sharding import Mesh
from jax.sharding import PartitionSpec as P

HEAD_DIM = 128
GROUP = 5
REQUESTS = 5
NEW_TOKENS = 448


ROPE_THETA = 1000000.0
NORM_EPS = 1e-06
NEG_LARGE = -1e30


def rotate(vectors, positions):
    half_dim = vectors.shape[-1] // 2
    exponent = jnp.arange(half_dim, dtype=jnp.int32).astype(jnp.float32) * (2.0 / vectors.shape[-1])
    frequency = 1.0 / ROPE_THETA**exponent
    angles = positions[:, None] * frequency[None, :]
    target = (positions.shape[0],) + (1,) * (vectors.ndim - 2) + (half_dim,)
    cos_table = jnp.cos(angles).reshape(target)
    sin_table = jnp.sin(angles).reshape(target)
    first_half = vectors[..., :half_dim]
    second_half = vectors[..., half_dim:]
    return jnp.concatenate(
        [
            first_half * cos_table - second_half * sin_table,
            second_half * cos_table + first_half * sin_table,
        ],
        -1,
    )


def token_positions(cached_len, fresh_len, first_row, row_count):
    rows_here = first_row + jnp.arange(row_count, dtype=jnp.int32)
    request = rows_here // NEW_TOKENS
    within = rows_here % NEW_TOKENS
    picked = request[:, None] == jnp.arange(REQUESTS, dtype=jnp.int32)[None, :]
    start_pos = jnp.sum(jnp.where(picked, cached_len[None, :], 0), 1)
    live_count = jnp.sum(jnp.where(picked, fresh_len[None, :], 0), 1)
    return (start_pos + within, within < live_count)


def finish_rows(projected, cached_len, fresh_len, first_row):
    row_count = projected.shape[0]
    groups_here = projected.shape[1] // ((GROUP + 2) * HEAD_DIM)
    shaped = projected.reshape(row_count, groups_here, GROUP + 2, HEAD_DIM)
    positions, unused_live = token_positions(cached_len, fresh_len, first_row, row_count)
    angle_pos = positions.astype(jnp.float32)
    queries = rotate(shaped[:, :, :GROUP], angle_pos).astype(jnp.bfloat16).reshape(row_count, -1)
    new_keys = rotate(shaped[:, :, GROUP], angle_pos).astype(jnp.bfloat16).reshape(row_count, -1)
    new_values = shaped[:, :, GROUP + 1].astype(jnp.bfloat16).reshape(row_count, -1)
    return (queries, new_keys, new_values)


def append_rows(cache, new_rows, cached_len, fresh_len, first_slot):
    slot_count = cache.shape[1]
    slot_pos = first_slot + jnp.arange(slot_count, dtype=jnp.int32)
    offsets = slot_pos[None, :] - cached_len[:, None]
    is_live = (offsets >= 0) & (offsets < fresh_len[:, None])
    source_rows = jnp.arange(REQUESTS, dtype=jnp.int32)[:, None] * NEW_TOKENS + jnp.clip(
        offsets, 0, NEW_TOKENS - 1
    )
    return jnp.where(is_live[:, :, None], jnp.take(new_rows, source_rows, axis=0), cache)


GX = ("y", "zl", "x")
GY = ("zh", "c")


def gather_gx_chain(value):
    for axis in GX[::-1]:
        value = lax.all_gather(value, axis, axis=0, tiled=True)
    return value


def gather_gx(value):
    copies = lax.psum(1, GX)
    tiled = jnp.tile(value, (copies,) + (1,) * (value.ndim - 1))
    return lax.all_to_all(tiled, GX, 0, 0, tiled=True)


def psum_gx(value):
    for axis in GX[::-1]:
        value = lax.psum(value, axis)
    return value


def pmax_gx(value):
    for axis in GX[::-1]:
        value = lax.pmax(value, axis)
    return value


def share_rows(share_sum, cached_len, fresh_len, first_row):
    queries, new_keys, new_values = finish_rows(share_sum, cached_len, fresh_len, first_row)
    widths = (queries.shape[1], new_keys.shape[1])
    joined = gather_gx_chain(jnp.concatenate([queries, new_keys, new_values], axis=1))
    return (
        joined[:, : widths[0]],
        joined[:, widths[0] : widths[0] + widths[1]],
        joined[:, widths[0] + widths[1] :],
    )


def per_device(
    hidden,
    norm_gain,
    qkv_weight,
    qkv_bias,
    out_weight,
    key_cache,
    value_cache,
    cached_len,
    fresh_len,
):
    scale = HEAD_DIM ** (-0.5)
    token_count = REQUESTS * NEW_TOKENS
    gx_size = lax.psum(1, GX)
    model_width = hidden.shape[1] * gx_size
    hidden_f = hidden.astype(jnp.float32)
    gathered = lax.all_gather(hidden, GY, axis=0, tiled=True).astype(jnp.float32)
    squares = jnp.sum(gathered * gathered, axis=1, keepdims=True)
    gained = (gathered * norm_gain[None, :]).astype(jnp.bfloat16)
    bias_f = qkv_bias.astype(jnp.float32)[None, :]
    row_share = token_count // gx_size
    share_start = lax.axis_index(GX) * row_share
    partial = jnp.dot(gained, qkv_weight, preferred_element_type=jnp.float32)
    proj_width = partial.shape[1]
    pad = jnp.zeros((token_count, HEAD_DIM - 1), jnp.float32)
    payload = jnp.concatenate([partial, squares, pad], axis=1).astype(jnp.bfloat16)
    payload = lax.all_to_all(payload, GX, 0, 0, tiled=True).astype(jnp.float32)
    payload = jnp.sum(payload.reshape(gx_size, row_share, -1), axis=0)
    scale_row = lax.rsqrt(payload[:, proj_width : proj_width + 1] / model_width + NORM_EPS)
    summed = payload[:, :proj_width] * scale_row
    queries, new_keys, new_values = share_rows(summed + bias_f, cached_len, fresh_len, share_start)
    slot_count = key_cache.shape[1]
    first_slot = lax.axis_index(GX) * slot_count
    key_out = append_rows(key_cache, new_keys, cached_len, fresh_len, first_slot)
    value_out = append_rows(value_cache, new_values, cached_len, fresh_len, first_slot)
    groups_here = key_cache.shape[2] // HEAD_DIM
    query_blocks = queries.reshape(REQUESTS, NEW_TOKENS, groups_here, GROUP, HEAD_DIM)
    key_blocks = key_out.reshape(REQUESTS, slot_count, groups_here, HEAD_DIM)
    value_blocks = value_out.reshape(REQUESTS, slot_count, groups_here, HEAD_DIM)
    slot_pos = first_slot + jnp.arange(slot_count, dtype=jnp.int32)
    query_pos = jnp.arange(NEW_TOKENS, dtype=jnp.int32)

    total_len = (cached_len + fresh_len)[:, None, None]
    visible = (slot_pos[None, None, :] < total_len) & (
        slot_pos[None, None, :] <= cached_len[:, None, None] + query_pos[None, :, None]
    )
    scores = (
        jnp.einsum("rikgd,rpkd->rkgip", query_blocks, key_blocks, preferred_element_type=jnp.float32)
        * scale
    )
    scores = jnp.where(visible[:, None, None], scores, NEG_LARGE)
    top = jnp.max(scores, axis=4)
    top_hi = top.astype(jnp.bfloat16)
    top_lo = (top - top_hi.astype(jnp.float32)).astype(jnp.bfloat16)
    top_here = top_hi.astype(jnp.float32) + top_lo.astype(jnp.float32)
    weighted = jnp.where(visible[:, None, None], jnp.exp(scores - top_here[..., None]), 0.0)
    denom = jnp.sum(weighted, axis=4)
    mixed = jnp.einsum(
        "rkgip,rpkd->rikgd",
        weighted.astype(jnp.bfloat16),
        value_blocks,
        preferred_element_type=jnp.float32,
    )

    def per_token(stat):
        return stat.transpose(0, 3, 1, 2).reshape(token_count, -1)

    stats = jnp.concatenate(
        [
            per_token(top_hi.astype(jnp.float32)),
            per_token(top_lo.astype(jnp.float32)),
            per_token(denom),
        ],
        axis=1,
    )
    mixed = mixed.reshape(token_count, -1)
    stats = stats.reshape(token_count, -1)
    mixed_width = mixed.shape[1]
    heads_here = mixed_width // HEAD_DIM
    pad = jnp.zeros((token_count, HEAD_DIM - stats.shape[1]), jnp.float32)
    both = jnp.concatenate([mixed, stats, pad], axis=1).astype(jnp.bfloat16)
    both = lax.all_to_all(both, GX, 0, 0, tiled=True)
    both = both.reshape(gx_size, row_share, -1)
    part_stats = both[:, :, mixed_width : mixed_width + 3 * heads_here].astype(jnp.float32)
    part_top = part_stats[:, :, :heads_here] + part_stats[:, :, heads_here : 2 * heads_here]
    part_denom = part_stats[:, :, 2 * heads_here :]
    top_all = jnp.max(part_top, axis=0)
    scale_k = jnp.exp(part_top - top_all[None])
    denom = jnp.sum(part_denom * scale_k, axis=0)
    weight_k = scale_k / denom[None]
    parts = both[:, :, :mixed_width].reshape(gx_size, row_share, heads_here, HEAD_DIM)
    mixed = jnp.sum(parts.astype(jnp.float32) * weight_k[..., None], axis=0)
    unused_pos, is_live = token_positions(cached_len, fresh_len, share_start, row_share)
    ratio = mixed
    attended = jnp.where(is_live[:, None], ratio.reshape(row_share, -1), 0.0).astype(jnp.bfloat16)
    partial_out = jnp.dot(
        gather_gx(attended),
        out_weight,
        preferred_element_type=jnp.float32,
    )
    gy_size = lax.psum(1, GY)
    summed_out = lax.all_to_all(partial_out.astype(jnp.bfloat16), GY, 0, 0, tiled=True)
    summed_out = jnp.sum(summed_out.astype(jnp.float32).reshape(gy_size, token_count // gy_size, -1), axis=0)
    output = (hidden_f + summed_out).astype(jnp.bfloat16)
    return (output, key_out, value_out)


def solution(mesh):
    sub_mesh = Mesh(
        mesh.devices.reshape(4, mesh.shape["gx"] // 16, 4, mesh.shape["gy"] // 2, 2), GX + GY
    )
    in_specs = (
        P(GY, GX),
        P(GX),
        P(GX, GY),
        P(GY),
        P(GY, GX),
        P(None, GX, GY),
        P(None, GX, GY),
        P(),
        P(),
    )
    out_specs = (P(GY, GX), P(None, GX, GY), P(None, GX, GY))
    return jax.shard_map(
        per_device, mesh=sub_mesh, in_specs=in_specs, out_specs=out_specs, check_vma=False
    )
```

```python
import jax
import jax.numpy as jnp
from jax import lax
from jax.sharding import Mesh
from jax.sharding import PartitionSpec as P

HEAD_DIM = 128
GROUP = 5
REQUESTS = 5
NEW_TOKENS = 448


ROPE_THETA = 1000000.0
NORM_EPS = 1e-06
NEG_LARGE = -1e30


def rotate(vectors, positions):
    half_dim = vectors.shape[-1] // 2
    exponent = jnp.arange(half_dim, dtype=jnp.int32).astype(jnp.float32) * (2.0 / vectors.shape[-1])
    frequency = 1.0 / ROPE_THETA**exponent
    angles = positions[:, None] * frequency[None, :]
    target = (positions.shape[0],) + (1,) * (vectors.ndim - 2) + (half_dim,)
    cos_table = jnp.cos(angles).reshape(target)
    sin_table = jnp.sin(angles).reshape(target)
    first_half = vectors[..., :half_dim]
    second_half = vectors[..., half_dim:]
    return jnp.concatenate(
        [
            first_half * cos_table - second_half * sin_table,
            second_half * cos_table + first_half * sin_table,
        ],
        -1,
    )


def token_positions(cached_len, fresh_len, first_row, row_count):
    rows_here = first_row + jnp.arange(row_count, dtype=jnp.int32)
    request = rows_here // NEW_TOKENS
    within = rows_here % NEW_TOKENS
    picked = request[:, None] == jnp.arange(REQUESTS, dtype=jnp.int32)[None, :]
    start_pos = jnp.sum(jnp.where(picked, cached_len[None, :], 0), 1)
    live_count = jnp.sum(jnp.where(picked, fresh_len[None, :], 0), 1)
    return (start_pos + within, within < live_count)


def finish_rows(projected, cached_len, fresh_len, first_row):
    row_count = projected.shape[0]
    groups_here = projected.shape[1] // ((GROUP + 2) * HEAD_DIM)
    shaped = projected.reshape(row_count, groups_here, GROUP + 2, HEAD_DIM)
    positions, unused_live = token_positions(cached_len, fresh_len, first_row, row_count)
    angle_pos = positions.astype(jnp.float32)
    queries = rotate(shaped[:, :, :GROUP], angle_pos).astype(jnp.bfloat16).reshape(row_count, -1)
    new_keys = rotate(shaped[:, :, GROUP], angle_pos).astype(jnp.bfloat16).reshape(row_count, -1)
    new_values = shaped[:, :, GROUP + 1].astype(jnp.bfloat16).reshape(row_count, -1)
    return (queries, new_keys, new_values)


def append_rows(cache, new_rows, cached_len, fresh_len, first_slot):
    slot_count = cache.shape[1]
    slot_pos = first_slot + jnp.arange(slot_count, dtype=jnp.int32)
    offsets = slot_pos[None, :] - cached_len[:, None]
    is_live = (offsets >= 0) & (offsets < fresh_len[:, None])
    source_rows = jnp.arange(REQUESTS, dtype=jnp.int32)[:, None] * NEW_TOKENS + jnp.clip(
        offsets, 0, NEW_TOKENS - 1
    )
    return jnp.where(is_live[:, :, None], jnp.take(new_rows, source_rows, axis=0), cache)


GX = ("y", "zl", "x")
GY = ("zh", "c")


def gather_gx_chain(value):
    for axis in GX[:0:-1]:
        value = lax.all_gather(value, axis, axis=0, tiled=True)
    copies = lax.psum(1, GX[0])
    tiled = jnp.tile(value, (copies,) + (1,) * (value.ndim - 1))
    return lax.all_to_all(tiled, GX[0], 0, 0, tiled=True)


def gather_gx(value):
    copies = lax.psum(1, GX)
    tiled = jnp.tile(value, (copies,) + (1,) * (value.ndim - 1))
    return lax.all_to_all(tiled, GX, 0, 0, tiled=True)


def psum_gx(value):
    for axis in GX[::-1]:
        value = lax.psum(value, axis)
    return value


def pmax_gx(value):
    for axis in GX[::-1]:
        value = lax.pmax(value, axis)
    return value


def share_rows(share_sum, cached_len, fresh_len, first_row):
    queries, new_keys, new_values = finish_rows(share_sum, cached_len, fresh_len, first_row)
    widths = (queries.shape[1], new_keys.shape[1])
    joined = gather_gx_chain(jnp.concatenate([queries, new_keys, new_values], axis=1))
    return (
        joined[:, : widths[0]],
        joined[:, widths[0] : widths[0] + widths[1]],
        joined[:, widths[0] + widths[1] :],
    )


def per_device(
    hidden,
    norm_gain,
    qkv_weight,
    qkv_bias,
    out_weight,
    key_cache,
    value_cache,
    cached_len,
    fresh_len,
):
    scale = HEAD_DIM ** (-0.5)
    token_count = REQUESTS * NEW_TOKENS
    gx_size = lax.psum(1, GX)
    model_width = hidden.shape[1] * gx_size
    hidden_f = hidden.astype(jnp.float32)
    gathered = lax.all_gather(hidden, GY, axis=0, tiled=True).astype(jnp.float32)
    squares = jnp.sum(gathered * gathered, axis=1, keepdims=True)
    gained = (gathered * norm_gain[None, :]).astype(jnp.bfloat16)
    bias_f = qkv_bias.astype(jnp.float32)[None, :]
    row_share = token_count // gx_size
    share_start = lax.axis_index(GX) * row_share
    partial = jnp.dot(gained, qkv_weight, preferred_element_type=jnp.float32)
    proj_width = partial.shape[1]
    pad = jnp.zeros((token_count, HEAD_DIM - 1), jnp.float32)
    payload = jnp.concatenate([partial, squares, pad], axis=1).astype(jnp.bfloat16)
    payload = lax.all_to_all(payload, GX, 0, 0, tiled=True).astype(jnp.float32)
    payload = jnp.sum(payload.reshape(gx_size, row_share, -1), axis=0)
    scale_row = lax.rsqrt(payload[:, proj_width : proj_width + 1] / model_width + NORM_EPS)
    summed = payload[:, :proj_width] * scale_row
    queries, new_keys, new_values = share_rows(summed + bias_f, cached_len, fresh_len, share_start)
    slot_count = key_cache.shape[1]
    first_slot = lax.axis_index(GX) * slot_count
    key_out = append_rows(key_cache, new_keys, cached_len, fresh_len, first_slot)
    value_out = append_rows(value_cache, new_values, cached_len, fresh_len, first_slot)
    groups_here = key_cache.shape[2] // HEAD_DIM
    query_blocks = queries.reshape(REQUESTS, NEW_TOKENS, groups_here, GROUP, HEAD_DIM)
    key_blocks = key_out.reshape(REQUESTS, slot_count, groups_here, HEAD_DIM)
    value_blocks = value_out.reshape(REQUESTS, slot_count, groups_here, HEAD_DIM)
    slot_pos = first_slot + jnp.arange(slot_count, dtype=jnp.int32)
    query_pos = jnp.arange(NEW_TOKENS, dtype=jnp.int32)

    total_len = (cached_len + fresh_len)[:, None, None]
    visible = (slot_pos[None, None, :] < total_len) & (
        slot_pos[None, None, :] <= cached_len[:, None, None] + query_pos[None, :, None]
    )
    scores = (
        jnp.einsum("rikgd,rpkd->rkgip", query_blocks, key_blocks, preferred_element_type=jnp.float32)
        * scale
    )
    scores = jnp.where(visible[:, None, None], scores, NEG_LARGE)
    top = jnp.max(scores, axis=4)
    top_hi = top.astype(jnp.bfloat16)
    top_lo = (top - top_hi.astype(jnp.float32)).astype(jnp.bfloat16)
    top_here = top_hi.astype(jnp.float32) + top_lo.astype(jnp.float32)
    weighted = jnp.where(visible[:, None, None], jnp.exp(scores - top_here[..., None]), 0.0)
    denom = jnp.sum(weighted, axis=4)
    mixed = jnp.einsum(
        "rkgip,rpkd->rikgd",
        weighted.astype(jnp.bfloat16),
        value_blocks,
        preferred_element_type=jnp.float32,
    )

    def per_token(stat):
        return stat.transpose(0, 3, 1, 2).reshape(token_count, -1)

    stats = jnp.concatenate(
        [
            per_token(top_hi.astype(jnp.float32)),
            per_token(top_lo.astype(jnp.float32)),
            per_token(denom),
        ],
        axis=1,
    )
    mixed = mixed.reshape(token_count, -1)
    stats = stats.reshape(token_count, -1)
    mixed_width = mixed.shape[1]
    heads_here = mixed_width // HEAD_DIM
    pad = jnp.zeros((token_count, HEAD_DIM - stats.shape[1]), jnp.float32)
    both = jnp.concatenate([mixed, stats, pad], axis=1).astype(jnp.bfloat16)
    both = lax.all_to_all(both, GX, 0, 0, tiled=True)
    both = both.reshape(gx_size, row_share, -1)
    part_stats = both[:, :, mixed_width : mixed_width + 3 * heads_here].astype(jnp.float32)
    part_top = part_stats[:, :, :heads_here] + part_stats[:, :, heads_here : 2 * heads_here]
    part_denom = part_stats[:, :, 2 * heads_here :]
    top_all = jnp.max(part_top, axis=0)
    scale_k = jnp.exp(part_top - top_all[None])
    denom = jnp.sum(part_denom * scale_k, axis=0)
    weight_k = scale_k / denom[None]
    parts = both[:, :, :mixed_width].reshape(gx_size, row_share, heads_here, HEAD_DIM)
    mixed = jnp.sum(parts.astype(jnp.float32) * weight_k[..., None], axis=0)
    unused_pos, is_live = token_positions(cached_len, fresh_len, share_start, row_share)
    ratio = mixed
    attended = jnp.where(is_live[:, None], ratio.reshape(row_share, -1), 0.0).astype(jnp.bfloat16)
    partial_out = jnp.dot(
        gather_gx(attended),
        out_weight,
        preferred_element_type=jnp.float32,
    )
    gy_size = lax.psum(1, GY)
    summed_out = lax.all_to_all(partial_out.astype(jnp.bfloat16), GY, 0, 0, tiled=True)
    summed_out = jnp.sum(summed_out.astype(jnp.float32).reshape(gy_size, token_count // gy_size, -1), axis=0)
    output = (hidden_f + summed_out).astype(jnp.bfloat16)
    return (output, key_out, value_out)


def solution(mesh):
    sub_mesh = Mesh(
        mesh.devices.reshape(4, mesh.shape["gx"] // 16, 4, mesh.shape["gy"] // 2, 2), GX + GY
    )
    in_specs = (
        P(GY, GX),
        P(GX),
        P(GX, GY),
        P(GY),
        P(GY, GX),
        P(None, GX, GY),
        P(None, GX, GY),
        P(),
        P(),
    )
    out_specs = (P(GY, GX), P(None, GX, GY), P(None, GX, GY))
    return jax.shard_map(
        per_device, mesh=sub_mesh, in_specs=in_specs, out_specs=out_specs, check_vma=False
    )
```

```python
import jax
import jax.numpy as jnp
from jax import lax
from jax.sharding import Mesh
from jax.sharding import PartitionSpec as P

HEAD_DIM = 128
GROUP = 5
REQUESTS = 5
NEW_TOKENS = 448


ROPE_THETA = 1000000.0
NORM_EPS = 1e-06
NEG_LARGE = -1e30


def rotate(vectors, positions):
    half_dim = vectors.shape[-1] // 2
    exponent = jnp.arange(half_dim, dtype=jnp.int32).astype(jnp.float32) * (2.0 / vectors.shape[-1])
    frequency = 1.0 / ROPE_THETA**exponent
    angles = positions[:, None] * frequency[None, :]
    target = (positions.shape[0],) + (1,) * (vectors.ndim - 2) + (half_dim,)
    cos_table = jnp.cos(angles).reshape(target)
    sin_table = jnp.sin(angles).reshape(target)
    first_half = vectors[..., :half_dim]
    second_half = vectors[..., half_dim:]
    return jnp.concatenate(
        [
            first_half * cos_table - second_half * sin_table,
            second_half * cos_table + first_half * sin_table,
        ],
        -1,
    )


def token_positions(cached_len, fresh_len, first_row, row_count):
    rows_here = first_row + jnp.arange(row_count, dtype=jnp.int32)
    request = rows_here // NEW_TOKENS
    within = rows_here % NEW_TOKENS
    picked = request[:, None] == jnp.arange(REQUESTS, dtype=jnp.int32)[None, :]
    start_pos = jnp.sum(jnp.where(picked, cached_len[None, :], 0), 1)
    live_count = jnp.sum(jnp.where(picked, fresh_len[None, :], 0), 1)
    return (start_pos + within, within < live_count)


def finish_rows(projected, cached_len, fresh_len, first_row):
    row_count = projected.shape[0]
    groups_here = projected.shape[1] // ((GROUP + 2) * HEAD_DIM)
    shaped = projected.reshape(row_count, groups_here, GROUP + 2, HEAD_DIM)
    positions, unused_live = token_positions(cached_len, fresh_len, first_row, row_count)
    angle_pos = positions.astype(jnp.float32)
    queries = rotate(shaped[:, :, :GROUP], angle_pos).astype(jnp.bfloat16).reshape(row_count, -1)
    new_keys = rotate(shaped[:, :, GROUP], angle_pos).astype(jnp.bfloat16).reshape(row_count, -1)
    new_values = shaped[:, :, GROUP + 1].astype(jnp.bfloat16).reshape(row_count, -1)
    return (queries, new_keys, new_values)


def append_rows(cache, new_rows, cached_len, fresh_len, first_slot):
    slot_count = cache.shape[1]
    slot_pos = first_slot + jnp.arange(slot_count, dtype=jnp.int32)
    offsets = slot_pos[None, :] - cached_len[:, None]
    is_live = (offsets >= 0) & (offsets < fresh_len[:, None])
    source_rows = jnp.arange(REQUESTS, dtype=jnp.int32)[:, None] * NEW_TOKENS + jnp.clip(
        offsets, 0, NEW_TOKENS - 1
    )
    return jnp.where(is_live[:, :, None], jnp.take(new_rows, source_rows, axis=0), cache)


GX = ("y", "zl", "x")
GY = ("zh", "c")


def gather_gx_chain(value):
    for axis in GX[::-1]:
        value = lax.all_gather(value, axis, axis=0, tiled=True)
    return value


def gather_gx(value):
    copies = lax.psum(1, GX)
    tiled = jnp.tile(value, (copies,) + (1,) * (value.ndim - 1))
    return lax.all_to_all(tiled, GX, 0, 0, tiled=True)


def psum_gx(value):
    for axis in GX[::-1]:
        value = lax.psum(value, axis)
    return value


def pmax_gx(value):
    for axis in GX[::-1]:
        value = lax.pmax(value, axis)
    return value


def share_rows(share_sum, cached_len, fresh_len, first_row):
    queries, new_keys, new_values = finish_rows(share_sum, cached_len, fresh_len, first_row)
    widths = (queries.shape[1], new_keys.shape[1])
    joined = gather_gx_chain(jnp.concatenate([queries, new_keys, new_values], axis=1))
    return (
        joined[:, : widths[0]],
        joined[:, widths[0] : widths[0] + widths[1]],
        joined[:, widths[0] + widths[1] :],
    )


def per_device(
    hidden,
    norm_gain,
    qkv_weight,
    qkv_bias,
    out_weight,
    key_cache,
    value_cache,
    cached_len,
    fresh_len,
):
    scale = HEAD_DIM ** (-0.5)
    token_count = REQUESTS * NEW_TOKENS
    gx_size = lax.psum(1, GX)
    model_width = hidden.shape[1] * gx_size
    hidden_f = hidden.astype(jnp.float32)
    gy_copies = lax.psum(1, GY)
    gathered = lax.all_to_all(jnp.tile(hidden, (gy_copies, 1)), GY, 0, 0, tiled=True)
    gathered = gathered.astype(jnp.float32)
    squares = jnp.sum(gathered * gathered, axis=1, keepdims=True)
    gained = (gathered * norm_gain[None, :]).astype(jnp.bfloat16)
    bias_f = qkv_bias.astype(jnp.float32)[None, :]
    row_share = token_count // gx_size
    share_start = lax.axis_index(GX) * row_share
    partial = jnp.dot(gained, qkv_weight, preferred_element_type=jnp.float32)
    proj_width = partial.shape[1]
    pad = jnp.zeros((token_count, HEAD_DIM - 1), jnp.float32)
    payload = jnp.concatenate([partial, squares, pad], axis=1).astype(jnp.bfloat16)
    payload = lax.all_to_all(payload, GX, 0, 0, tiled=True).astype(jnp.float32)
    payload = jnp.sum(payload.reshape(gx_size, row_share, -1), axis=0)
    scale_row = lax.rsqrt(payload[:, proj_width : proj_width + 1] / model_width + NORM_EPS)
    summed = payload[:, :proj_width] * scale_row
    queries, new_keys, new_values = share_rows(summed + bias_f, cached_len, fresh_len, share_start)
    slot_count = key_cache.shape[1]
    first_slot = lax.axis_index(GX) * slot_count
    key_out = append_rows(key_cache, new_keys, cached_len, fresh_len, first_slot)
    value_out = append_rows(value_cache, new_values, cached_len, fresh_len, first_slot)
    groups_here = key_cache.shape[2] // HEAD_DIM
    query_blocks = queries.reshape(REQUESTS, NEW_TOKENS, groups_here, GROUP, HEAD_DIM)
    key_blocks = key_out.reshape(REQUESTS, slot_count, groups_here, HEAD_DIM)
    value_blocks = value_out.reshape(REQUESTS, slot_count, groups_here, HEAD_DIM)
    slot_pos = first_slot + jnp.arange(slot_count, dtype=jnp.int32)
    query_pos = jnp.arange(NEW_TOKENS, dtype=jnp.int32)

    total_len = (cached_len + fresh_len)[:, None, None]
    visible = (slot_pos[None, None, :] < total_len) & (
        slot_pos[None, None, :] <= cached_len[:, None, None] + query_pos[None, :, None]
    )
    scores = (
        jnp.einsum("rikgd,rpkd->rkgip", query_blocks, key_blocks, preferred_element_type=jnp.float32)
        * scale
    )
    scores = jnp.where(visible[:, None, None], scores, NEG_LARGE)
    top = jnp.max(scores, axis=4)
    top_hi = top.astype(jnp.bfloat16)
    top_lo = (top - top_hi.astype(jnp.float32)).astype(jnp.bfloat16)
    top_here = top_hi.astype(jnp.float32) + top_lo.astype(jnp.float32)
    weighted = jnp.where(visible[:, None, None], jnp.exp(scores - top_here[..., None]), 0.0)
    denom = jnp.sum(weighted, axis=4)
    mixed = jnp.einsum(
        "rkgip,rpkd->rikgd",
        weighted.astype(jnp.bfloat16),
        value_blocks,
        preferred_element_type=jnp.float32,
    )

    def per_token(stat):
        return stat.transpose(0, 3, 1, 2).reshape(token_count, -1)

    stats = jnp.concatenate(
        [
            per_token(top_hi.astype(jnp.float32)),
            per_token(top_lo.astype(jnp.float32)),
            per_token(denom),
        ],
        axis=1,
    )
    mixed = mixed.reshape(token_count, -1)
    stats = stats.reshape(token_count, -1)
    mixed_width = mixed.shape[1]
    heads_here = mixed_width // HEAD_DIM
    pad = jnp.zeros((token_count, HEAD_DIM - stats.shape[1]), jnp.float32)
    both = jnp.concatenate([mixed, stats, pad], axis=1).astype(jnp.bfloat16)
    both = lax.all_to_all(both, GX, 0, 0, tiled=True)
    both = both.reshape(gx_size, row_share, -1)
    part_stats = both[:, :, mixed_width : mixed_width + 3 * heads_here].astype(jnp.float32)
    part_top = part_stats[:, :, :heads_here] + part_stats[:, :, heads_here : 2 * heads_here]
    part_denom = part_stats[:, :, 2 * heads_here :]
    top_all = jnp.max(part_top, axis=0)
    scale_k = jnp.exp(part_top - top_all[None])
    denom = jnp.sum(part_denom * scale_k, axis=0)
    weight_k = scale_k / denom[None]
    parts = both[:, :, :mixed_width].reshape(gx_size, row_share, heads_here, HEAD_DIM)
    mixed = jnp.sum(parts.astype(jnp.float32) * weight_k[..., None], axis=0)
    unused_pos, is_live = token_positions(cached_len, fresh_len, share_start, row_share)
    ratio = mixed
    attended = jnp.where(is_live[:, None], ratio.reshape(row_share, -1), 0.0).astype(jnp.bfloat16)
    partial_out = jnp.dot(
        gather_gx(attended),
        out_weight,
        preferred_element_type=jnp.float32,
    )
    gy_size = lax.psum(1, GY)
    summed_out = lax.all_to_all(partial_out.astype(jnp.bfloat16), GY, 0, 0, tiled=True)
    summed_out = jnp.sum(summed_out.astype(jnp.float32).reshape(gy_size, token_count // gy_size, -1), axis=0)
    output = (hidden_f + summed_out).astype(jnp.bfloat16)
    return (output, key_out, value_out)


def solution(mesh):
    sub_mesh = Mesh(
        mesh.devices.reshape(4, mesh.shape["gx"] // 16, 4, mesh.shape["gy"] // 2, 2), GX + GY
    )
    in_specs = (
        P(GY, GX),
        P(GX),
        P(GX, GY),
        P(GY),
        P(GY, GX),
        P(None, GX, GY),
        P(None, GX, GY),
        P(),
        P(),
    )
    out_specs = (P(GY, GX), P(None, GX, GY), P(None, GX, GY))
    return jax.shard_map(
        per_device, mesh=sub_mesh, in_specs=in_specs, out_specs=out_specs, check_vma=False
    )
```

```python
import jax
import jax.numpy as jnp
from jax import lax
from jax.sharding import Mesh
from jax.sharding import PartitionSpec as P

HEAD_DIM = 128
GROUP = 5
REQUESTS = 5
NEW_TOKENS = 448


ROPE_THETA = 1000000.0
NORM_EPS = 1e-06
NEG_LARGE = -1e30


def rotate(vectors, positions):
    half_dim = vectors.shape[-1] // 2
    exponent = jnp.arange(half_dim, dtype=jnp.int32).astype(jnp.float32) * (2.0 / vectors.shape[-1])
    frequency = 1.0 / ROPE_THETA**exponent
    angles = positions[:, None] * frequency[None, :]
    target = (positions.shape[0],) + (1,) * (vectors.ndim - 2) + (half_dim,)
    cos_table = jnp.cos(angles).reshape(target)
    sin_table = jnp.sin(angles).reshape(target)
    first_half = vectors[..., :half_dim]
    second_half = vectors[..., half_dim:]
    return jnp.concatenate(
        [
            first_half * cos_table - second_half * sin_table,
            second_half * cos_table + first_half * sin_table,
        ],
        -1,
    )


def token_positions(cached_len, fresh_len, first_row, row_count):
    rows_here = first_row + jnp.arange(row_count, dtype=jnp.int32)
    request = rows_here // NEW_TOKENS
    within = rows_here % NEW_TOKENS
    picked = request[:, None] == jnp.arange(REQUESTS, dtype=jnp.int32)[None, :]
    start_pos = jnp.sum(jnp.where(picked, cached_len[None, :], 0), 1)
    live_count = jnp.sum(jnp.where(picked, fresh_len[None, :], 0), 1)
    return (start_pos + within, within < live_count)


def finish_rows(projected, cached_len, fresh_len, first_row):
    row_count = projected.shape[0]
    groups_here = projected.shape[1] // ((GROUP + 2) * HEAD_DIM)
    shaped = projected.reshape(row_count, groups_here, GROUP + 2, HEAD_DIM)
    positions, unused_live = token_positions(cached_len, fresh_len, first_row, row_count)
    angle_pos = positions.astype(jnp.float32)
    queries = rotate(shaped[:, :, :GROUP], angle_pos).astype(jnp.bfloat16).reshape(row_count, -1)
    new_keys = rotate(shaped[:, :, GROUP], angle_pos).astype(jnp.bfloat16).reshape(row_count, -1)
    new_values = shaped[:, :, GROUP + 1].astype(jnp.bfloat16).reshape(row_count, -1)
    return (queries, new_keys, new_values)


def append_rows(cache, new_rows, cached_len, fresh_len, first_slot):
    slot_count = cache.shape[1]
    slot_pos = first_slot + jnp.arange(slot_count, dtype=jnp.int32)
    offsets = slot_pos[None, :] - cached_len[:, None]
    is_live = (offsets >= 0) & (offsets < fresh_len[:, None])
    source_rows = jnp.arange(REQUESTS, dtype=jnp.int32)[:, None] * NEW_TOKENS + jnp.clip(
        offsets, 0, NEW_TOKENS - 1
    )
    return jnp.where(is_live[:, :, None], jnp.take(new_rows, source_rows, axis=0), cache)


GX = ("y", "zl", "x")
GY = ("zh", "c")


def gather_gx_chain(value):
    for axis in GX[::-1]:
        value = lax.all_gather(value, axis, axis=0, tiled=True)
    return value


def gather_gx(value):
    copies = lax.psum(1, GX)
    tiled = jnp.tile(value, (copies,) + (1,) * (value.ndim - 1))
    return lax.all_to_all(tiled, GX, 0, 0, tiled=True)


def psum_gx(value):
    for axis in GX[::-1]:
        value = lax.psum(value, axis)
    return value


def pmax_gx(value):
    for axis in GX[::-1]:
        value = lax.pmax(value, axis)
    return value


def share_rows(share_sum, cached_len, fresh_len, first_row):
    queries, new_keys, new_values = finish_rows(share_sum, cached_len, fresh_len, first_row)
    widths = (queries.shape[1], new_keys.shape[1])
    joined = gather_gx_chain(jnp.concatenate([queries, new_keys, new_values], axis=1))
    return (
        joined[:, : widths[0]],
        joined[:, widths[0] : widths[0] + widths[1]],
        joined[:, widths[0] + widths[1] :],
    )


def per_device(
    hidden,
    norm_gain,
    qkv_weight,
    qkv_bias,
    out_weight,
    key_cache,
    value_cache,
    cached_len,
    fresh_len,
):
    scale = HEAD_DIM ** (-0.5)
    token_count = REQUESTS * NEW_TOKENS
    gx_size = lax.psum(1, GX)
    model_width = hidden.shape[1] * gx_size
    hidden_f = hidden.astype(jnp.float32)
    gathered = lax.all_gather(hidden, GY, axis=0, tiled=True).astype(jnp.float32)
    squares = jnp.sum(gathered * gathered, axis=1, keepdims=True)
    gained = (gathered * norm_gain[None, :]).astype(jnp.bfloat16)
    bias_f = qkv_bias.astype(jnp.float32)[None, :]
    row_share = token_count // gx_size
    share_start = lax.axis_index(GX) * row_share
    partial = jnp.dot(gained, qkv_weight, preferred_element_type=jnp.float32)
    proj_width = partial.shape[1]
    pad = jnp.zeros((token_count, HEAD_DIM - 1), jnp.float32)
    payload = jnp.concatenate([partial, squares, pad], axis=1).astype(jnp.bfloat16)
    payload = lax.all_to_all(payload, GX, 0, 0, tiled=True).astype(jnp.float32)
    payload = jnp.sum(payload.reshape(gx_size, row_share, -1), axis=0)
    scale_row = lax.rsqrt(payload[:, proj_width : proj_width + 1] / model_width + NORM_EPS)
    summed = payload[:, :proj_width] * scale_row
    queries, new_keys, new_values = share_rows(summed + bias_f, cached_len, fresh_len, share_start)
    slot_count = key_cache.shape[1]
    first_slot = lax.axis_index(GX) * slot_count
    key_out = append_rows(key_cache, new_keys, cached_len, fresh_len, first_slot)
    value_out = append_rows(value_cache, new_values, cached_len, fresh_len, first_slot)
    groups_here = key_cache.shape[2] // HEAD_DIM
    query_blocks = queries.reshape(REQUESTS, NEW_TOKENS, groups_here, GROUP, HEAD_DIM)
    key_blocks = key_out.reshape(REQUESTS, slot_count, groups_here, HEAD_DIM)
    value_blocks = value_out.reshape(REQUESTS, slot_count, groups_here, HEAD_DIM)
    slot_pos = first_slot + jnp.arange(slot_count, dtype=jnp.int32)
    query_pos = jnp.arange(NEW_TOKENS, dtype=jnp.int32)

    total_len = (cached_len + fresh_len)[:, None, None]
    visible = (slot_pos[None, None, :] < total_len) & (
        slot_pos[None, None, :] <= cached_len[:, None, None] + query_pos[None, :, None]
    )
    scores = (
        jnp.einsum("rikgd,rpkd->rkgip", query_blocks, key_blocks, preferred_element_type=jnp.float32)
        * scale
    )
    scores = jnp.where(visible[:, None, None], scores, NEG_LARGE)
    top = jnp.max(scores, axis=4)
    top_hi = top.astype(jnp.bfloat16)
    top_lo = (top - top_hi.astype(jnp.float32)).astype(jnp.bfloat16)
    top_here = top_hi.astype(jnp.float32) + top_lo.astype(jnp.float32)
    weighted = jnp.where(visible[:, None, None], jnp.exp(scores - top_here[..., None]), 0.0)
    denom = jnp.sum(weighted, axis=4)
    mixed = jnp.einsum(
        "rkgip,rpkd->rikgd",
        weighted.astype(jnp.bfloat16),
        value_blocks,
        preferred_element_type=jnp.float32,
    )

    def per_token(stat):
        return stat.transpose(0, 3, 1, 2).reshape(token_count, -1)

    stats = jnp.concatenate(
        [
            per_token(top_hi.astype(jnp.float32)),
            per_token(top_lo.astype(jnp.float32)),
            per_token(denom),
        ],
        axis=1,
    )
    mixed = mixed.reshape(token_count, -1)
    stats = stats.reshape(token_count, -1)
    mixed_width = mixed.shape[1]
    heads_here = mixed_width // HEAD_DIM
    pad = jnp.zeros((token_count, HEAD_DIM - stats.shape[1]), jnp.float32)
    both = jnp.concatenate([mixed, stats, pad], axis=1).astype(jnp.bfloat16)
    both = lax.all_to_all(both, GX, 0, 0, tiled=True)
    both = both.reshape(gx_size, row_share, -1)
    part_stats = both[:, :, mixed_width : mixed_width + 3 * heads_here].astype(jnp.float32)
    part_top = part_stats[:, :, :heads_here] + part_stats[:, :, heads_here : 2 * heads_here]
    part_denom = part_stats[:, :, 2 * heads_here :]
    top_all = jnp.max(part_top, axis=0)
    scale_k = jnp.exp(part_top - top_all[None])
    denom = jnp.sum(part_denom * scale_k, axis=0)
    weight_k = scale_k / denom[None]
    parts = both[:, :, :mixed_width].reshape(gx_size, row_share, heads_here, HEAD_DIM)
    mixed = jnp.sum(parts.astype(jnp.float32) * weight_k[..., None], axis=0)
    unused_pos, is_live = token_positions(cached_len, fresh_len, share_start, row_share)
    ratio = mixed
    attended = jnp.where(is_live[:, None], ratio.reshape(row_share, -1), 0.0).astype(jnp.bfloat16)
    partial_out = jnp.dot(
        gather_gx(attended),
        out_weight,
        preferred_element_type=jnp.float32,
    )
    gy_size = lax.psum(1, GY)
    core_size = lax.psum(1, GY[1])
    out_rows = token_count // gy_size
    staged = partial_out.reshape(gy_size // core_size, core_size, out_rows, -1).transpose(1, 0, 2, 3)
    staged = lax.all_to_all(staged.astype(jnp.bfloat16), GY[1], 0, 0, tiled=True)
    staged = jnp.sum(staged.astype(jnp.float32), axis=0)
    staged = lax.all_to_all(staged.astype(jnp.bfloat16), GY[0], 0, 0, tiled=True)
    summed_out = jnp.sum(staged.astype(jnp.float32), axis=0)
    output = (hidden_f + summed_out).astype(jnp.bfloat16)
    return (output, key_out, value_out)


def solution(mesh):
    sub_mesh = Mesh(
        mesh.devices.reshape(4, mesh.shape["gx"] // 16, 4, mesh.shape["gy"] // 2, 2), GX + GY
    )
    in_specs = (
        P(GY, GX),
        P(GX),
        P(GX, GY),
        P(GY),
        P(GY, GX),
        P(None, GX, GY),
        P(None, GX, GY),
        P(),
        P(),
    )
    out_specs = (P(GY, GX), P(None, GX, GY), P(None, GX, GY))
    return jax.shard_map(
        per_device, mesh=sub_mesh, in_specs=in_specs, out_specs=out_specs, check_vma=False
    )
```
